32 devices in a mesh: section: 4 (over z), dp: 2 (over x), tensor: 4 (over y, core).
Axes of the slice: x: 2, y: 2, z: 4, core: 2. Of those that a mesh axis runs over, the one named last changes fastest.
Arguments:
- sent: bfloat16 [8, 384, 6144], P('section', 'dp', 'tensor'), may hold values from -6 to 6
- stashed_inputs: bfloat16 [16, 96, 6144], P('section', 'dp', 'tensor'), may hold values from -6 to 6
- table: int32 [4, 4], P('section'), may hold values from 0 to 3, each once within a row
- embedded: bfloat16 [384, 6144], P('dp', 'tensor'), may hold values from -6 to 6
- loss_gradient: bfloat16 [384, 6144], P('dp', 'tensor'), may hold values from -6 to 6
- weight: bfloat16 [4, 6144, 6144], P('section', None, 'tensor'), may hold values from -0.078125 to 0.078125
- adapter_down_weight: bfloat16 [4, 6144, 128], P('section'), may hold values from -0.078125 to 0.078125
- adapter_up_weight: bfloat16 [4, 128, 6144], P('section', None, 'tensor'), may hold values from -0.5 to 0.5
Outputs:
- forward_output: bfloat16 [4, 384, 6144], P('section', 'dp', 'tensor')
- backward_output: bfloat16 [4, 384, 6144], P('section', 'dp', 'tensor')
- down_gradient: bfloat16 [4, 6144, 128], P('section', 'tensor')
- up_gradient: bfloat16 [4, 128, 6144], P('section', None, 'tensor')
The draws below stay inside these ranges and needn't reach their ends.
Inputs may be any that keep to these rules, and one draw needn't show every extreme that they name: Each row of table is a permutation of 0 to 3.
All inputs are finite; a program needn't handle non-finite values.
Results may differ from the reference program's by a relative error of at most 0.019.
Values may be sent and summed in bfloat16 or wider, within the bound.
A program may use at most 64 MiB of HBM per device.

```python
import jax
import jax.numpy as jnp
from jax import lax

MODEL_WIDTH = 6144
ADAPTER_RANK = 128
TOK_DEV = 192
TOKENS = 384
PIECE = 48
N_SECTION = 4
N_DP = 2
N_TENSOR = 4


def block_scale(own_key, dims, split, least, top_value):
    def one(dim, blocks):
        steps = jax.random.uniform(jax.random.fold_in(jax.random.fold_in(own_key, 6), dim), (blocks,), jnp.float32, least / len(split), top_value / len(split))
        return jnp.repeat(jnp.exp(steps), dims[dim] // blocks).reshape((-1,) + (1,) * (len(dims) - dim - 1))

    factor_of = one(*split[0])
    for cut in split[1:]:
        factor_of = factor_of * one(*cut)
    return factor_of


def normal_values(stream_key, extent, width, reach, pieces=(), kind=jnp.bfloat16):
    drawn = width * jax.random.normal(stream_key, extent, jnp.float32)
    if pieces:
        drawn = drawn * block_scale(stream_key, extent, pieces, -0.22, 0.18)
    return jnp.clip(drawn, -reach, reach).astype(kind)


def setup_inputs(seed: int = 0) -> dict:
    keys = jax.random.split(jax.random.key(seed), 9)
    return {
        "sent": normal_values(keys[0], (2 * N_SECTION, TOKENS, MODEL_WIDTH), 1.0, 6.0, ((0, 4), (1, 2), (2, 4))),
        "stashed_inputs": normal_values(keys[1], (N_SECTION * N_SECTION, PIECE * N_DP, MODEL_WIDTH), 1.0, 6.0, ((0, 4), (1, 2), (2, 4))),
        "table": jax.vmap(lambda own: jax.random.permutation(own, N_SECTION))(jax.random.split(keys[2], N_SECTION)).reshape((N_SECTION, N_SECTION)).astype(jnp.int32),
        "embedded": normal_values(keys[3], (TOKENS, MODEL_WIDTH), 1.0, 6.0, ((0, 2), (1, 4))),
        "loss_gradient": normal_values(keys[4], (TOKENS, MODEL_WIDTH), 1.0, 6.0, ((0, 2), (1, 4))),
        "weight": normal_values(keys[5], (N_SECTION, MODEL_WIDTH, MODEL_WIDTH), MODEL_WIDTH ** -0.5, 0.078125, ((0, 4), (2, 4))),
        "adapter_down_weight": normal_values(keys[6], (N_SECTION, MODEL_WIDTH, ADAPTER_RANK), MODEL_WIDTH ** -0.5, 0.078125, ((0, 4),)),
        "adapter_up_weight": normal_values(keys[7], (N_SECTION, ADAPTER_RANK, MODEL_WIDTH), ADAPTER_RANK ** -0.5, 0.5, ((0, 4), (2, 4))),
    }


coef = 0.7978845608028654


def gelu_pair(u):
    inner = coef * (u + 0.044715 * u * u * u)
    tanh_v = jnp.tanh(inner)
    value = 0.5 * u * (1.0 + tanh_v)
    slope = 0.5 * (1.0 + tanh_v) + 0.5 * u * (1.0 - tanh_v * tanh_v) * coef * (1.0 + 3.0 * 0.044715 * u * u)
    return value, slope


def round_back(value):
    rounded = lax.optimization_barrier(value.astype(jnp.bfloat16))
    return rounded.astype(jnp.float32)


def single_section(items):
    x_a, g_b, x_b, w_section, down_matrix, up = items
    h_a = jnp.dot(x_a, down_matrix, preferred_element_type=jnp.float32).astype(jnp.bfloat16)
    u_a = jnp.dot(x_a, w_section, preferred_element_type=jnp.float32) + jnp.dot(h_a, up, preferred_element_type=jnp.float32)
    value_a, unused = gelu_pair(u_a)
    y_a = (x_a.astype(jnp.float32) + value_a).astype(jnp.bfloat16)
    h_b = jnp.dot(x_b, down_matrix, preferred_element_type=jnp.float32).astype(jnp.bfloat16)
    u_b = jnp.dot(x_b, w_section, preferred_element_type=jnp.float32) + jnp.dot(h_b, up, preferred_element_type=jnp.float32)
    unused_b, slope_b = gelu_pair(u_b)
    scaled = (g_b.astype(jnp.float32) * slope_b).astype(jnp.bfloat16)
    scaled_parts = scaled.reshape(TOKENS, N_TENSOR, MODEL_WIDTH // N_TENSOR).astype(jnp.float32)
    w_parts = w_section.reshape(MODEL_WIDTH, N_TENSOR, MODEL_WIDTH // N_TENSOR).astype(jnp.float32)
    up_parts = up.reshape(ADAPTER_RANK, N_TENSOR, MODEL_WIDTH // N_TENSOR).astype(jnp.float32)
    low_parts = round_back(jnp.einsum('rtc,ktc->trk', scaled_parts, up_parts))
    low_terms = jnp.einsum('trk,dk->trd', low_parts, down_matrix.astype(jnp.float32))
    partial_value = jnp.einsum('rtc,dtc->trd', scaled_parts, w_parts) + low_terms
    input_grad = jnp.sum(round_back(partial_value), axis=0)
    low_grad = jnp.dot(scaled, up.T, preferred_element_type=jnp.float32).astype(jnp.bfloat16)
    dx_b = (g_b.astype(jnp.float32) + input_grad).astype(jnp.bfloat16)
    xb_rep = x_b.reshape(N_DP, TOK_DEV, MODEL_WIDTH).astype(jnp.float32)
    lg_rep = low_grad.reshape(N_DP, TOK_DEV, ADAPTER_RANK).astype(jnp.float32)
    hb_rep = h_b.reshape(N_DP, TOK_DEV, ADAPTER_RANK).astype(jnp.float32)
    sb_rep = scaled.reshape(N_DP, TOK_DEV, MODEL_WIDTH).astype(jnp.float32)
    down_part = jnp.einsum('rtd,rtk->rdk', xb_rep, lg_rep)
    up_part = jnp.einsum('rtk,rtd->rkd', hb_rep, sb_rep)
    down_gradient = jnp.sum(round_back(down_part), axis=0).astype(jnp.bfloat16)
    up_gradient = jnp.sum(round_back(up_part), axis=0).astype(jnp.bfloat16)
    return y_a, dx_b, down_gradient, up_gradient


def reference(sent, stashed_inputs, table, embedded, loss_gradient, weight, adapter_down_weight, adapter_up_weight):
    pairs = sent.reshape(N_SECTION, 2, TOKENS, MODEL_WIDTH)
    forward_input = jnp.concatenate([embedded[None], pairs[:-1, 1]], axis=0)
    incoming_gradient = jnp.concatenate([pairs[1:, 0], loss_gradient[None]], axis=0)
    inverse = jnp.argsort(table, axis=1).astype(jnp.int32)
    blocks = stashed_inputs.reshape(N_SECTION, N_SECTION, N_DP, PIECE, MODEL_WIDTH)
    holders = jnp.broadcast_to(jnp.arange(N_SECTION, dtype=jnp.int32)[None, :], (N_SECTION, N_SECTION))
    picked = blocks[holders, inverse.T]
    backward_input = jnp.transpose(picked, (0, 2, 1, 3, 4)).reshape(N_SECTION, TOKENS, MODEL_WIDTH)
    forward_output, backward_output, down_gradient, up_gradient = lax.map(single_section, (forward_input, incoming_gradient, backward_input, weight, adapter_down_weight, adapter_up_weight))
    return forward_output, backward_output, down_gradient, up_gradient
```

```python
import functools

import jax
import jax.numpy as jnp
from jax import lax
from jax.experimental import pallas as pl
from jax.experimental.pallas import tpu as pltpu
from jax.sharding import PartitionSpec as P

coef = 0.7978845608028654


def shifted(block, axis, distance):
    devices = range(lax.axis_size(axis))
    route = [(i - distance, i) for i in devices if i - distance in devices]
    return lax.ppermute(block, axis, route)


def gelu_pair(u):
    inner = coef * (u + 0.044715 * u * u * u)
    tanh_v = jnp.tanh(inner)
    value = 0.5 * u * (1.0 + tanh_v)
    slope = 0.5 * (1.0 + tanh_v) + 0.5 * u * (1.0 - tanh_v * tanh_v) * coef * (
        1.0 + 3.0 * 0.044715 * u * u
    )
    return (value, slope)


def on_device(
    sent,
    stashed_inputs,
    table,
    embedded,
    loss_gradient,
    weight,
    adapter_down_weight,
    adapter_up_weight,
):
    section = lax.axis_index("section")
    sections = lax.axis_size("section")
    w_section = weight[0]
    down_matrix = adapter_down_weight[0]
    up_matrix = adapter_up_weight[0]
    below = shifted(sent[1], "section", 1)
    above = shifted(sent[0], "section", -1)
    forward_input = jnp.where(section == 0, embedded, below)
    incoming_gradient = jnp.where(section == sections - 1, loss_gradient, above)
    order = jnp.argsort(table[0])
    arranged = jnp.take(stashed_inputs, order, axis=0)
    fetched = lax.all_to_all(arranged, "section", split_axis=0, concat_axis=0, tiled=True)
    backward_input = fetched.reshape(-1, fetched.shape[-1])
    full_a, full_b = (
        lax.all_gather(forward_input, "tensor", axis=1, tiled=True),
        lax.all_gather(backward_input, "tensor", axis=1, tiled=True),
    )
    main_a = jnp.dot(full_a, w_section, preferred_element_type=jnp.float32)
    h_a = jnp.dot(full_a, down_matrix, preferred_element_type=jnp.float32).astype(jnp.bfloat16)
    u_a = main_a + jnp.dot(h_a, up_matrix, preferred_element_type=jnp.float32)
    value_a, unused = gelu_pair(u_a)
    forward_output = (forward_input.astype(jnp.float32) + value_a).astype(jnp.bfloat16)
    h_b = jnp.dot(full_b, down_matrix, preferred_element_type=jnp.float32).astype(jnp.bfloat16)
    u_b = jnp.dot(full_b, w_section, preferred_element_type=jnp.float32) + jnp.dot(
        h_b, up_matrix, preferred_element_type=jnp.float32
    )
    unused_b, slope_b = gelu_pair(u_b)
    scaled = (incoming_gradient.astype(jnp.float32) * slope_b).astype(jnp.bfloat16)
    low_part = lax.dot_general(
        scaled, up_matrix, (((1,), (1,)), ((), ())), preferred_element_type=jnp.float32
    )
    low_piece = low_part.astype(jnp.bfloat16)
    partial_value = lax.dot_general(
        scaled, w_section, (((1,), (1,)), ((), ())), preferred_element_type=jnp.float32
    )
    partial_value = partial_value + lax.dot_general(
        low_piece, down_matrix, (((1,), (1,)), ((), ())), preferred_element_type=jnp.float32
    )
    input_grad = lax.psum_scatter(
        partial_value.astype(jnp.bfloat16), "tensor", scatter_dimension=1, tiled=True
    ).astype(jnp.float32)
    backward_output = (incoming_gradient.astype(jnp.float32) + input_grad).astype(jnp.bfloat16)
    low_grad = lax.psum(low_part.astype(jnp.bfloat16), "tensor")
    down_term = lax.dot_general(
        backward_input, low_grad, (((0,), (0,)), ((), ())), preferred_element_type=jnp.float32
    )
    up_term = lax.dot_general(
        h_b, scaled, (((0,), (0,)), ((), ())), preferred_element_type=jnp.float32
    )
    down_sum, up_sum = (
        lax.psum(down_term.astype(jnp.bfloat16), "dp").astype(jnp.float32),
        lax.psum(up_term.astype(jnp.bfloat16), "dp").astype(jnp.float32),
    )
    down_gradient = down_sum.astype(jnp.bfloat16)
    up_gradient = up_sum.astype(jnp.bfloat16)
    return (forward_output[None], backward_output[None], down_gradient[None], up_gradient[None])


F32 = jnp.float32
BF16 = jnp.bfloat16
MESH = pl.DeviceIdType.MESH


def dot_nn(a, b):
    return lax.dot_general(a, b, (((1,), (0,)), ((), ())), preferred_element_type=F32)


def dot_nt(a, b):
    return lax.dot_general(a, b, (((1,), (1,)), ((), ())), preferred_element_type=F32)


def dot_tn(a, b):
    return lax.dot_general(a, b, (((0,), (0,)), ((), ())), preferred_element_type=F32)


def stash_order(s, S):
    return sorted(range(S), key=lambda k: (abs(k - s), k))


def link_order(s, S):
    b = [("b", k) for k in stash_order(s, S)]
    a = [("a", c) for c in range(S)]
    if s == 0:
        mixed = [b[0]]
        for k in range(1, S):
            mixed += [a[k - 1], b[k]]
        return mixed + a[S - 1:]
    if s == S - 1:
        return b[:2] + a[:S - 1] + b[2:] + a[S - 1:]
    return b + a


def up_order(s, S):
    b = [("b", k) for k in range(s + 1, S)]
    a = [("a", c) for c in range(S)] if s < S - 1 else []
    if 0 < s < S - 2:
        return b[:1] + a[:2] + b[1:] + a[2:]
    return b + a


def relay_slots(s, S):
    order = link_order(s, S)
    last_b = max(i for i, item in enumerate(order) if item[0] == "b")
    slots = [[], [], [], []]
    for i in range(last_b + 1):
        slots[0].append(("p", order[i]))
        if i:
            slots[0].append(("q", order[i - 1]))
    rest = order[last_b + 1:]
    now = len(rest) if s == 0 else 1
    slots[1] += [("p", item) for item in rest[:now]]
    slots[1].append(("q", order[last_b]))
    sent = rest[:now]
    late = []
    for item in rest[now:]:
        if 0 < s < S - 1 and s != 1 and item == rest[-1]:
            late.append(item)
            continue
        slots[2].append(("p", item))
        slots[2].append(("q", sent.pop(0)))
        sent.append(item)
    slots[3] += [("p", item) for item in late]
    tail = [("q", item) for item in sent + late]
    return slots + [tail]


def window_kernel(
    sections, tile, part,
    sent, stash_hbm, table, embedded, loss, weight, down, up,
    out_f, out_b, out_d, out_u,
    stash_v, w, dn, upv, xa, xb, g, arranged, u, ua, scaled, low, low_in, pair, pair_in, lg, lg_in, hb, ha,
    p_send, q_send, o_send, p_recv, q_recv, o_recv, own,
    du_send, du_recv, xo,
    w_sem, d_sem, loc_sem, ex_s, ex_r, az_s, az_r, gz_s, gz_r,
    xo_s, xo_r, y_s, y_r, c_s, c_r, f_s, f_r, low_s, low_r, p_s, p_r, q_s, q_r, o_s, o_r, dp_s, dp_r,
):
    S = sections
    s = lax.axis_index("section")
    d = lax.axis_index("dp")
    t = lax.axis_index("tensor")
    t1 = t + 1 - 2 * (t % 2)
    t2 = (t + 2) % 4
    t3 = (t1 + 2) % 4
    rel = [t, t1, t2, t3]
    piece, cols = stash_v.shape[1], stash_v.shape[2]
    rows = S * piece
    tiles = cols // tile
    parts = cols // part
    stash_copy = pltpu.make_async_copy(stash_hbm, stash_v, loc_sem.at[0])
    stash_copy.start()

    def remote(src, dst, ss, rs, **device):
        return pltpu.make_async_remote_copy(
            src_ref=src, dst_ref=dst, send_sem=ss, recv_sem=rs,
            device_id=device, device_id_type=MESH)

    emb_copy = pltpu.make_async_copy(embedded, xa.at[0], loc_sem.at[3])
    loss_copy = pltpu.make_async_copy(loss, g, loc_sem.at[1])
    up_copy = pltpu.make_async_copy(up, upv, loc_sem.at[2])
    w_copies = [pltpu.make_async_copy(weight.at[rel[r]], w.at[r], w_sem.at[r]) for r in range(4)]
    d_copies = [pltpu.make_async_copy(down.at[rel[r]], dn.at[r], d_sem.at[r]) for r in range(4)]

    barrier = pltpu.get_barrier_semaphore()
    for j in range(1, S):
        pl.semaphore_signal(barrier, inc=1, device_id={"section": (s + j) % S}, device_id_type=MESH)
    for r in range(1, 4):
        pl.semaphore_signal(barrier, inc=1, device_id={"tensor": rel[r]}, device_id_type=MESH)
    pl.semaphore_signal(barrier, inc=1, device_id={"dp": 1 - d}, device_id_type=MESH)

    @pl.when(s == 0)
    def _():
        emb_copy.start()

    stash_copy.wait()
    for j in range(S):
        dest = (s + j) % S
        k = jnp.int32(0)
        for i in range(S):
            k = jnp.where(table[0, i] == dest, i, k)
        if j == 0:
            xb[0, s] = stash_v[k]
        else:
            arranged[j] = stash_v[k]
    pl.semaphore_wait(barrier, S + 3)

    def ex(v, to):
        return remote(arranged.at[(to - v) % S], xb.at[0, v], ex_s.at[to], ex_r.at[v], section=to)

    def az(v, c):
        return remote(sent.at[1, c], xa.at[0, c], az_s.at[c], az_r.at[c], section=(v + 1) % S)

    gz = remote(sent.at[0], g, gz_s.at[0], gz_r.at[0], section=(s + S - 1) % S)

    def hop_y(item):
        x, k, at = (xb, item[1], item[1]) if item[0] == "b" else (xa, item[1], S + item[1])
        return remote(x.at[0, k], x.at[2, k], y_s.at[at], y_r.at[at], tensor=t2)

    def hop_c(item):
        x, k, at = (xb, item[1], item[1]) if item[0] == "b" else (xa, item[1], S + item[1])
        return remote(x.at[0, k], x.at[1, k], c_s.at[at], c_r.at[at], tensor=t1)

    def hop_f(item):
        x, k, at = (xb, item[1], item[1]) if item[0] == "b" else (xa, item[1], S + item[1])
        return remote(x.at[2, k], x.at[3, k], f_s.at[at], f_r.at[at], tensor=t1)

    def hop_x(k):
        return remote(xb.at[0, k], xo.at[k], xo_s.at[k], xo_r.at[k], dp=1 - d)

    def act(v, step):
        kind, item = step
        if kind == "q":
            hop_y(item).wait_recv()
            hop_f(item).start()
            return
        if item[0] == "b":
            if item[1] != v:
                ex(item[1], v).wait_recv()
        elif v == 0:
            if item[1] == 0:
                emb_copy.wait()
        else:
            az(v - 1, item[1]).wait_recv()
        hop_y(item).start()
        hop_c(item).start()
        if item[0] == "b":
            hop_x(item[1]).start()

    def per_section(run):
        for v in range(S):
            pl.when(s == v)(functools.partial(run, v))

    def relay(slot):
        def run(v):
            for step in relay_slots(v, S)[slot]:
                act(v, step)
        per_section(run)

    def first_sends(v):
        act(v, ("p", ("b", v)))
        for k in range(v - 1, -1, -1):
            ex(v, k).start()
        for kind, k in up_order(v, S):
            if kind == "b":
                ex(v, k).start()
            else:
                az(v, k).start()
        if v > 0:
            gz.start()
        if v == S - 1:
            loss_copy.start()
    per_section(first_sends)

    for r in range(4):
        d_copies[r].start()
        w_copies[r].start()
    up_copy.start()

    def run_rest(v):
        for step in relay_slots(v, S)[0][1:]:
            act(v, step)
    per_section(run_rest)

    def forward(x, r, acc):
        for n in range(tiles):
            val = dot_nn(x[r].reshape(rows, cols), w[r, :, pl.ds(n * tile, tile)])
            acc[n] = val if r == 0 else acc[n] + val

    def low_of(x, r):
        return dot_nn(x[r].reshape(rows, cols), dn[r])

    d_copies[0].wait()
    w_copies[0].wait()
    forward(xb, 0, u)
    h = low_of(xb, 0)
    for k in range(S):
        hop_c(("b", k)).wait_recv()
    d_copies[1].wait()
    w_copies[1].wait()
    forward(xb, 1, u)
    h = h + low_of(xb, 1)
    relay(1)
    d_copies[2].wait()
    w_copies[2].wait()
    forward(xb, 2, u)
    h = h + low_of(xb, 2)
    for k in range(S):
        hop_f(("b", k)).wait_recv()
    d_copies[3].wait()
    w_copies[3].wait()
    forward(xb, 3, u)
    h = h + low_of(xb, 3)
    hb[...] = h.astype(BF16)
    up_copy.wait()

    def slope_body(n, carry):
        at = pl.ds(pl.multiple_of(n * tile, tile), tile)
        unused, slope = gelu_pair(u[n] + dot_nn(hb[...], upv[:, at]))
        u[n] = slope
        return carry
    lax.fori_loop(0, tiles, slope_body, 0)
    relay(2)

    @pl.when(s == S - 1)
    def _():
        loss_copy.wait()

    @pl.when(s < S - 1)
    def _():
        gz.wait_recv()

    def scale_body(n, carry):
        at = pl.ds(pl.multiple_of(n * tile, tile), tile)
        scaled[:, at] = (g[:, :, at].reshape(rows, tile).astype(F32) * u[n]).astype(BF16)
        return carry
    lax.fori_loop(0, tiles, scale_body, 0)

    low_copy = remote(low, low_in, low_s.at[0], low_r.at[0], tensor=t1)
    pair_copy = remote(pair, pair_in, low_s.at[1], low_r.at[1], tensor=t2)

    def partial(r, n):
        return dot_nt(scaled[...], w[r, pl.ds(n * part, part), :])

    def p_copy(n):
        return remote(p_send.at[n], p_recv.at[n], p_s.at[n], p_r.at[n], tensor=t1)

    def q_copy(n):
        return remote(q_send.at[n], q_recv.at[n], q_s.at[n], q_r.at[n], tensor=t2)

    def o_copy(n):
        return remote(o_send.at[n], o_recv.at[n], o_s.at[n], o_r.at[n], tensor=t1)

    def p_step(n):
        p_send[n] = partial(3, n).astype(BF16)
        p_copy(n).start()

    def q_step(n):
        mine = partial(2, n)
        p_copy(n).wait_recv()
        q_send[n] = (mine + p_recv[n].astype(F32)).astype(BF16)
        q_copy(n).start()

    low[...] = dot_nt(scaled[...], upv[...]).astype(BF16)
    low_copy.start()
    p_step(0)
    p_step(1)
    low_copy.wait_recv()
    pair[...] = (low[...].astype(F32) + low_in[...].astype(F32)).astype(BF16)
    pair_copy.start()
    q_step(0)
    relay(3)
    for n in range(2, parts):
        p_step(n)
        q_step(n - 1)
    q_step(parts - 1)

    du_send[...] = dot_tn(hb[...], scaled[...]).astype(BF16)
    pair_copy.wait_recv()
    lg[...] = (pair[...].astype(F32) + pair_in[...].astype(F32)).astype(BF16)
    dd = remote(lg, lg_in, dp_s.at[1], dp_r.at[1], dp=1 - d)
    dd.start()
    du = remote(du_send, du_recv, dp_s.at[0], dp_r.at[0], dp=1 - d)
    du.start()

    forward(xa, 0, ua)
    h = low_of(xa, 0)
    for c in range(S):
        hop_c(("a", c)).wait_recv()
    forward(xa, 1, ua)
    h = h + low_of(xa, 1)
    relay(4)

    for n in range(parts):
        o_send[n] = partial(1, n).astype(BF16)
        o_copy(n).start()
    for n in range(parts):
        own[n] = partial(0, n) + dot_nt(lg[...], dn[0, pl.ds(n * part, part), :])

    forward(xa, 2, ua)
    h = h + low_of(xa, 2)
    for c in range(S):
        hop_f(("a", c)).wait_recv()
    forward(xa, 3, ua)
    h = h + low_of(xa, 3)
    ha[...] = h.astype(BF16)

    def out_body(n, carry):
        at = pl.ds(pl.multiple_of(n * tile, tile), tile)
        value, unused = gelu_pair(ua[n] + dot_nn(ha[...], upv[:, at]))
        base = xa[0, :, :, at].reshape(rows, tile).astype(F32)
        out_f[:, at] = (base + value).astype(BF16)
        return carry
    lax.fori_loop(0, tiles, out_body, 0)

    for k in range(S):
        hop_x(k).wait_recv()
    dd.wait_recv()
    here = dot_tn(xb[0].reshape(rows, cols), lg[...]).astype(BF16)
    there = dot_tn(xo[...].reshape(rows, cols), lg_in[...]).astype(BF16)
    out_d[...] = (here.astype(F32) + there.astype(F32)).astype(BF16)

    du.wait_recv()
    out_u[...] = (du_send[...].astype(F32) + du_recv[...].astype(F32)).astype(BF16)

    for n in range(parts):
        o_copy(n).wait_recv()
        q_copy(n).wait_recv()
        at = pl.ds(n * part, part)
        total = own[n] + o_recv[n].astype(F32) + q_recv[n].astype(F32)
        out_b[:, at] = (g[:, :, at].reshape(rows, part).astype(F32) + total).astype(BF16)

    def drain(v):
        for k in range(S):
            if k != v:
                ex(v, k).wait_send()
        if v < S - 1:
            for c in range(S):
                az(v, c).wait_send()
        if v > 0:
            gz.wait_send()
    per_section(drain)
    for k in range(S):
        hop_x(k).wait_send()
        for item in (("b", k), ("a", k)):
            hop_y(item).wait_send()
            hop_c(item).wait_send()
            hop_f(item).wait_send()
    low_copy.wait_send()
    pair_copy.wait_send()
    for n in range(parts):
        p_copy(n).wait_send()
        q_copy(n).wait_send()
        o_copy(n).wait_send()
    du.wait_send()
    dd.wait_send()


def fused_on_device(sent, stash, table, embedded, loss, weight, down, up):
    S = lax.axis_size("section")
    piece, cols = stash.shape[1], stash.shape[2]
    rows, rank = S * piece, up.shape[1]
    tile = next(k for k in (768, 512, 256, 128) if cols % k == 0)
    part = next(k for k in (384, 256, 128) if cols % k == 0)
    tiles, parts = cols // tile, cols // part
    hbm = pl.BlockSpec(memory_space=pltpu.HBM)
    vmem = pl.BlockSpec(memory_space=pltpu.VMEM)
    smem = pl.BlockSpec(memory_space=pltpu.SMEM)
    V = pltpu.VMEM
    dma = lambda *shape: pltpu.SemaphoreType.DMA(shape)
    block = (tiles, rows, tile)
    cut = (parts, rows, part)
    slim = V((rows, rank), BF16)
    stack = V((S, piece, cols), BF16)
    outs = pl.pallas_call(
        functools.partial(window_kernel, S, tile, part),
        out_shape=(
            jax.ShapeDtypeStruct((rows, cols), BF16),
            jax.ShapeDtypeStruct((rows, cols), BF16),
            jax.ShapeDtypeStruct((cols, rank), BF16),
            jax.ShapeDtypeStruct((rank, cols), BF16),
        ),
        in_specs=[hbm, hbm, smem, hbm, hbm, hbm, hbm, hbm],
        out_specs=(vmem,) * 4,
        scratch_shapes=[
            stack, V((4, cols, cols), BF16), V((4, cols, rank), BF16), V((rank, cols), BF16),
            V((4, S, piece, cols), BF16), V((4, S, piece, cols), BF16),
            stack, stack,
            V(block, F32), V(block, F32), V((rows, cols), BF16),
            slim, slim, slim, slim, slim, slim, slim, slim,
            V(cut, BF16), V(cut, BF16), V(cut, BF16),
            V(cut, BF16), V(cut, BF16), V(cut, BF16), V(cut, F32),
            V((rank, cols), BF16), V((rank, cols), BF16), stack,
            dma(4), dma(4), dma(4), dma(S), dma(S), dma(S), dma(S), dma(1), dma(1), dma(S), dma(S),
            dma(2 * S), dma(2 * S), dma(2 * S), dma(2 * S), dma(2 * S), dma(2 * S), dma(2), dma(2),
            dma(parts), dma(parts), dma(parts), dma(parts), dma(parts), dma(parts),
            dma(2), dma(2),
        ],
        compiler_params=pltpu.CompilerParams(
            collective_id=0, has_side_effects=True, vmem_limit_bytes=60 * 1024 * 1024),
    )(
        sent.reshape(2, S, piece, cols), stash, table,
        embedded.reshape(S, piece, cols), loss.reshape(S, piece, cols),
        weight.reshape(4, cols, cols), down.reshape(4, cols, rank), up[0],
    )
    return tuple(o[None] for o in outs)


def solution(mesh):
    placed = (
        P("section", "dp", "tensor"),
        P("section", "dp", "tensor"),
        P("section", None),
        P("dp", "tensor"),
        P("dp", "tensor"),
        P("section", None, "tensor"),
        P("section", None, None),
        P("section", None, "tensor"),
    )
    def program(*args):
        rows = args[1].shape[1] // mesh.shape["dp"]
        cols = args[1].shape[2] // mesh.shape["tensor"]
        fits = (
            mesh.shape["tensor"] == 4 and mesh.shape["dp"] == 2
            and rows % 16 == 0 and cols % 128 == 0
        )
        return sharded(fused_on_device if fits else on_device)(*args)

    def sharded(body):
      return jax.shard_map(
        body,
        mesh=mesh,
        in_specs=placed,
        out_specs=(
            P("section", "dp", "tensor"),
            P("section", "dp", "tensor"),
            P("section", "tensor", None),
            P("section", None, "tensor"),
        ),
        check_vma=False,
    )

    return program
```

```python
import functools

import jax
import jax.numpy as jnp
from jax import lax
from jax.experimental import pallas as pl
from jax.experimental.pallas import tpu as pltpu
from jax.sharding import PartitionSpec as P

coef = 0.7978845608028654


def shifted(block, axis, distance):
    devices = range(lax.axis_size(axis))
    route = [(i - distance, i) for i in devices if i - distance in devices]
    return lax.ppermute(block, axis, route)


def gelu_pair(u):
    inner = coef * (u + 0.044715 * u * u * u)
    tanh_v = jnp.tanh(inner)
    value = 0.5 * u * (1.0 + tanh_v)
    slope = 0.5 * (1.0 + tanh_v) + 0.5 * u * (1.0 - tanh_v * tanh_v) * coef * (
        1.0 + 3.0 * 0.044715 * u * u
    )
    return (value, slope)


def on_device(
    sent,
    stashed_inputs,
    table,
    embedded,
    loss_gradient,
    weight,
    adapter_down_weight,
    adapter_up_weight,
):
    section = lax.axis_index("section")
    sections = lax.axis_size("section")
    w_section = weight[0]
    down_matrix = adapter_down_weight[0]
    up_matrix = adapter_up_weight[0]
    below = shifted(sent[1], "section", 1)
    above = shifted(sent[0], "section", -1)
    forward_input = jnp.where(section == 0, embedded, below)
    incoming_gradient = jnp.where(section == sections - 1, loss_gradient, above)
    order = jnp.argsort(table[0])
    arranged = jnp.take(stashed_inputs, order, axis=0)
    fetched = lax.all_to_all(arranged, "section", split_axis=0, concat_axis=0, tiled=True)
    backward_input = fetched.reshape(-1, fetched.shape[-1])
    full_a, full_b = (
        lax.all_gather(forward_input, "tensor", axis=1, tiled=True),
        lax.all_gather(backward_input, "tensor", axis=1, tiled=True),
    )
    main_a = jnp.dot(full_a, w_section, preferred_element_type=jnp.float32)
    h_a = jnp.dot(full_a, down_matrix, preferred_element_type=jnp.float32).astype(jnp.bfloat16)
    u_a = main_a + jnp.dot(h_a, up_matrix, preferred_element_type=jnp.float32)
    value_a, unused = gelu_pair(u_a)
    forward_output = (forward_input.astype(jnp.float32) + value_a).astype(jnp.bfloat16)
    h_b = jnp.dot(full_b, down_matrix, preferred_element_type=jnp.float32).astype(jnp.bfloat16)
    u_b = jnp.dot(full_b, w_section, preferred_element_type=jnp.float32) + jnp.dot(
        h_b, up_matrix, preferred_element_type=jnp.float32
    )
    unused_b, slope_b = gelu_pair(u_b)
    scaled = (incoming_gradient.astype(jnp.float32) * slope_b).astype(jnp.bfloat16)
    low_part = lax.dot_general(
        scaled, up_matrix, (((1,), (1,)), ((), ())), preferred_element_type=jnp.float32
    )
    low_piece = low_part.astype(jnp.bfloat16)
    partial_value = lax.dot_general(
        scaled, w_section, (((1,), (1,)), ((), ())), preferred_element_type=jnp.float32
    )
    partial_value = partial_value + lax.dot_general(
        low_piece, down_matrix, (((1,), (1,)), ((), ())), preferred_element_type=jnp.float32
    )
    input_grad = lax.psum_scatter(
        partial_value.astype(jnp.bfloat16), "tensor", scatter_dimension=1, tiled=True
    ).astype(jnp.float32)
    backward_output = (incoming_gradient.astype(jnp.float32) + input_grad).astype(jnp.bfloat16)
    low_grad = lax.psum(low_part.astype(jnp.bfloat16), "tensor")
    down_term = lax.dot_general(
        backward_input, low_grad, (((0,), (0,)), ((), ())), preferred_element_type=jnp.float32
    )
    up_term = lax.dot_general(
        h_b, scaled, (((0,), (0,)), ((), ())), preferred_element_type=jnp.float32
    )
    down_sum, up_sum = (
        lax.psum(down_term.astype(jnp.bfloat16), "dp").astype(jnp.float32),
        lax.psum(up_term.astype(jnp.bfloat16), "dp").astype(jnp.float32),
    )
    down_gradient = down_sum.astype(jnp.bfloat16)
    up_gradient = up_sum.astype(jnp.bfloat16)
    return (forward_output[None], backward_output[None], down_gradient[None], up_gradient[None])


F32 = jnp.float32
BF16 = jnp.bfloat16
MESH = pl.DeviceIdType.MESH


def dot_nn(a, b):
    return lax.dot_general(a, b, (((1,), (0,)), ((), ())), preferred_element_type=F32)


def dot_nt(a, b):
    return lax.dot_general(a, b, (((1,), (1,)), ((), ())), preferred_element_type=F32)


def dot_tn(a, b):
    return lax.dot_general(a, b, (((0,), (0,)), ((), ())), preferred_element_type=F32)


def stash_order(s, S):
    return sorted(range(S), key=lambda k: (abs(k - s), k))


def link_order(s, S):
    return [("b", k) for k in stash_order(s, S)] + [("a", c) for c in range(S)]


FOUR = {
    0: {
        0: ("a0", "~b1", "+b2", "b0'", "b1", "~b2", "+b3", "+a0", "a0'", "b1'", "a1", "+a1", "b2", "+a2", "b3",),
        1: ("b2'", "+a3",),
        2: ("b3'", "a2",),
        3: ("a3",),
        9: ("a1'",),
        10: ("a2'", "a3'",),
    },
    1: {
        0: ("~b2", "+b3", "b0", "b1'", "b2", "+g", "b0'", "+a0", "b3",),
        1: ("b2'", "+a1", "a0",),
        2: ("b3'", "+a2",),
        3: ("a1", "+a3",),
        5: ("a2", "a0'",),
        6: ("a3", "a1'",),
        9: ("a2'",),
        10: ("a3'",),
    },
    2: {
        0: ("~b3", "+a0", "~b1", "+b0", "b3", "b2'", "b1", "+g", "b3'", "b0", "+a1",),
        1: ("b1'", "+a2",),
        2: ("b0'", "+a3",),
        3: ("a0",),
        5: ("a1",),
        6: ("a0'",),
        7: ("a2",),
        8: ("a3",),
        9: ("a1'",),
        10: ("a2'",),
        11: ("a3'",),
    },
    3: {
        0: ("~b2", "+b1", "b3'", "b2", "+b0", "+g", "a0", "b2'", "b1", "a0'", "b0",),
        1: ("b1'",),
        2: ("b0'", "a1",),
        3: ("a2",),
        5: ("a3",),
        9: ("a1'",),
        10: ("a2'",),
        11: ("a3'",),
    },
}


def read_plan(words):
    plan = []
    for word in words:
        kind = "s" if word[0] == "+" else "w" if word[0] == "~" else "q" if word[-1] == "'" else "p"
        name = word.strip("+~'")
        plan.append((kind, (name[0], int(name[1:] or 0))))
    return plan


def first_targets(s, S):
    order = stash_order(s, S)[1:]
    held = [item[1] for kind, item in relay_slot(s, S, 0) if kind == "s" and item[0] == "b"]
    return [k for k in order if k not in held]


def relay_slot(s, S, slot):
    if S == 4:
        return read_plan(FOUR[s].get(slot, ()))
    order = link_order(s, S)[1:]
    if slot == 0:
        late = [("s", ("a", c)) for c in range(S) if s < S - 1] + [("s", ("g", 0))] * (s > 0)
        return [("p", item) for item in order if item[0] == "b"] + late
    if slot == 2:
        return [("q", ("b", k)) for k in range(S)]
    if slot == 5:
        return [(kind, item) for item in order if item[0] == "a" for kind in "pq"]
    return []


def window_kernel(
    sections, tile, part,
    sent, stash_hbm, table, embedded, loss, weight, down, up,
    keep_f, keep_b, keep_d, keep_u,
    out_f, out_b, out_d, out_u,
    stash_v, w, dn, upv, xab, g, arranged, u, ua, scaled, low, low_in, pair, pair_in, lg, lg_in, hb, ha,
    pqo_send, p_recv, q_recv, o_recv, own,
    du_send, du_recv, xo,
    w_sem, d_sem, loc_sem, keep_sem, ex_s, ex_r, az_s, az_r, gz_s, gz_r,
    xo_s, xo_r, hop_s, y_r, c_r, f_r, low_s, low_r, pqo_s, p_r, q_r, o_r, dp_s, dp_r,
):
    S = sections
    xa, xb = xab.at[0], xab.at[1]
    p_send, q_send, o_send = pqo_send.at[0], pqo_send.at[1], pqo_send.at[2]
    s = lax.axis_index("section")
    d = lax.axis_index("dp")
    t = lax.axis_index("tensor")
    t1 = t + 1 - 2 * (t % 2)
    t2 = (t + 2) % 4
    t3 = (t1 + 2) % 4
    rel = [t, t1, t2, t3]
    piece, cols = stash_v.shape[1], stash_v.shape[2]
    rows = S * piece
    tiles = cols // tile
    parts = cols // part
    stash_copy = pltpu.make_async_copy(stash_hbm, stash_v, loc_sem.at[0])
    stash_copy.start()

    def remote(src, dst, ss, rs, **device):
        return pltpu.make_async_remote_copy(
            src_ref=src, dst_ref=dst, send_sem=ss, recv_sem=rs,
            device_id=device, device_id_type=MESH)

    emb_copy = pltpu.make_async_copy(embedded, xa.at[0], loc_sem.at[3])
    loss_copy = pltpu.make_async_copy(loss, g, loc_sem.at[1])
    up_copy = pltpu.make_async_copy(up, upv, loc_sem.at[2])
    w_copies = [pltpu.make_async_copy(weight.at[rel[r]], w.at[r], w_sem.at[r]) for r in range(4)]
    d_copies = [pltpu.make_async_copy(down.at[rel[r]], dn.at[r], d_sem.at[0]) for r in range(4)]
    d_all = pltpu.make_async_copy(down, dn, d_sem.at[0])

    barrier = pltpu.get_barrier_semaphore()
    for j in range(1, S):
        pl.semaphore_signal(barrier, inc=1, device_id={"section": (s + j) % S}, device_id_type=MESH)
    for r in range(1, 4):
        pl.semaphore_signal(barrier, inc=1, device_id={"tensor": rel[r]}, device_id_type=MESH)
    pl.semaphore_signal(barrier, inc=1, device_id={"dp": 1 - d}, device_id_type=MESH)

    @pl.when(s == 0)
    def _():
        emb_copy.start()

    stash_copy.wait()
    for j in range(S):
        dest = (s + j) % S
        k = jnp.int32(0)
        for i in range(S):
            k = jnp.where(table[0, i] == dest, i, k)
        if j == 0:
            xb[0, s] = stash_v[k]
        else:
            arranged[j] = stash_v[k]
    pl.semaphore_wait(barrier, S + 3)

    def ex(v, to):
        return remote(arranged.at[(to - v) % S], xb.at[0, v], ex_s.at[to], ex_r.at[v], section=to)

    def az(v, c):
        return remote(sent.at[1, c], xa.at[0, c], az_s.at[0], az_r.at[c], section=(v + 1) % S)

    gz = remote(sent.at[0], g, gz_s.at[0], gz_r.at[0], section=(s + S - 1) % S)

    def place(item):
        kind = 1 if item[0] == "b" else 0
        return (xb if kind else xa), item[1], kind

    def hop_y(item):
        x, k, kind = place(item)
        return remote(x.at[0, k], x.at[2, k], hop_s.at[0], y_r.at[kind * S + k], tensor=t2)

    def hop_c(item):
        x, k, kind = place(item)
        return remote(x.at[0, k], x.at[1, k], hop_s.at[0], c_r.at[kind], tensor=t1)

    def hop_f(item):
        x, k, kind = place(item)
        return remote(x.at[2, k], x.at[3, k], hop_s.at[0], f_r.at[kind], tensor=t1)

    def all_c(x, kind):
        return remote(x.at[0], x.at[1], hop_s.at[0], c_r.at[kind], tensor=t1)

    def all_f(x, kind):
        return remote(x.at[2], x.at[3], hop_s.at[0], f_r.at[kind], tensor=t1)

    def hop_x(k):
        return remote(xb.at[0, k], xo.at[k], xo_s.at[0], xo_r.at[0], dp=1 - d)

    all_x = remote(xb.at[0], xo, xo_s.at[0], xo_r.at[0], dp=1 - d)

    def act(v, step):
        kind, item = step
        if kind in "sw":
            copy = gz if item[0] == "g" else az(v, item[1]) if item[0] == "a" else ex(v, item[1])
            copy.start() if kind == "s" else copy.wait_send()
            return
        if kind == "q":
            hop_y(item).wait_recv()
            hop_f(item).start()
            return
        if item[0] == "b":
            if item[1] != v:
                ex(item[1], v).wait_recv()
        elif v == 0:
            if item[1] == 0:
                emb_copy.wait()
        else:
            az(v - 1, item[1]).wait_recv()
        hop_y(item).start()
        hop_c(item).start()
        if item[0] == "b":
            hop_x(item[1]).start()

    def per_section(run):
        for v in range(S):
            pl.when(s == v)(functools.partial(run, v))

    def relay(slot):
        def run(v):
            for step in relay_slot(v, S, slot):
                act(v, step)
        per_section(run)

    def first_sends(v):
        act(v, ("p", ("b", v)))
        for k in first_targets(v, S):
            ex(v, k).start()
        if v == S - 1:
            loss_copy.start()
    per_section(first_sends)

    for r in range(4):
        d_copies[r].start()
        w_copies[r].start()
    up_copy.start()

    def run_rest(v):
        for step in relay_slot(v, S, 0):
            act(v, step)
    per_section(run_rest)

    def forward(x, r, acc):
        for n in range(tiles):
            val = dot_nn(x[r].reshape(rows, cols), w[r, :, pl.ds(n * tile, tile)])
            acc[n] = val if r == 0 else acc[n] + val

    def low_of(x, r):
        return dot_nn(x[r].reshape(rows, cols), dn[r])

    d_all.wait()
    w_copies[0].wait()
    forward(xb, 0, u)
    h = low_of(xb, 0)
    relay(1)
    all_c(xb, 1).wait_recv()
    w_copies[1].wait()
    forward(xb, 1, u)
    h = h + low_of(xb, 1)
    relay(2)
    w_copies[2].wait()
    forward(xb, 2, u)
    h = h + low_of(xb, 2)
    relay(3)
    all_f(xb, 1).wait_recv()
    w_copies[3].wait()
    forward(xb, 3, u)
    h = h + low_of(xb, 3)
    hb[...] = h.astype(BF16)
    relay(4)
    up_copy.wait()

    def slope_body(n, carry):
        at = pl.ds(pl.multiple_of(n * tile, tile), tile)
        unused, slope = gelu_pair(u[n] + dot_nn(hb[...], upv[:, at]))
        u[n] = slope
        return carry
    lax.fori_loop(0, tiles, slope_body, 0)
    relay(5)
    relay(6)

    def near_blocks():
        forward(xa, 0, ua)
        all_c(xa, 0).wait_recv()
        forward(xa, 1, ua)
    early = (s > 0) & (s < S // 2)
    pl.when(early)(near_blocks)
    relay(7)

    @pl.when(s == S - 1)
    def _():
        loss_copy.wait()

    @pl.when(s < S - 1)
    def _():
        gz.wait_recv()

    def scale_body(n, carry):
        at = pl.ds(pl.multiple_of(n * tile, tile), tile)
        scaled[:, at] = (g[:, :, at].reshape(rows, tile).astype(F32) * u[n]).astype(BF16)
        return carry
    lax.fori_loop(0, tiles, scale_body, 0)

    low_copy = remote(low, low_in, low_s.at[0], low_r.at[0], tensor=t1)
    share = rows // 2
    lower = pl.ds(pl.multiple_of((t % 2) * share, share), share)
    pair_copy = remote(pair.at[lower], pair_in.at[lower], low_s.at[1], low_r.at[1], tensor=t2)
    pair_hop = remote(pair_in.at[lower], pair_in.at[lower], low_s.at[2], low_r.at[2], tensor=t1)

    def partial(r, n):
        return dot_nt(scaled[...], w[r, pl.ds(n * part, part), :])

    def p_copy(n):
        return remote(p_send.at[n], p_recv.at[n], pqo_s.at[0], p_r.at[(n >= lead) + (n >= parts - lead)], tensor=t1)

    def p_group(group):
        at = pl.ds(group[0], len(group))
        which = (group[0] >= lead) + (group[0] >= parts - lead)
        return remote(p_send.at[at], p_recv.at[at], pqo_s.at[0], p_r.at[which], tensor=t1)

    def q_copy(n):
        return remote(q_send.at[n], q_recv.at[n], pqo_s.at[0], q_r.at[n], tensor=t2)

    def o_copy(n):
        return remote(o_send.at[n], o_recv.at[n], pqo_s.at[0], o_r.at[0], tensor=t1)

    lead = max(parts // 4, 1)
    first, second, third = range(lead), range(lead, parts - lead), range(parts - lead, parts)

    def p_step(group):
        for n in group:
            p_send[n] = partial(3, n).astype(BF16)
        for n in group:
            p_copy(n).start()

    def q_step(group):
        for n in group:
            own[n] = partial(2, n)
        p_group(group).wait_recv()
        for n in group:
            q_send[n] = (own[n] + p_recv[n].astype(F32)).astype(BF16)
        for n in group:
            q_copy(n).start()

    p_step(first)
    low[...] = dot_nt(scaled[...], upv[...]).astype(BF16)
    low_copy.start()
    relay(8)
    q_step(first)
    relay(9)
    p_step(second)
    du_send[...] = dot_tn(hb[...], scaled[...]).astype(BF16)
    du = remote(du_send, du_recv, dp_s.at[0], dp_r.at[0], dp=1 - d)
    du.start()
    low_copy.wait_recv()
    pair[...] = (low[...].astype(F32) + low_in[...].astype(F32)).astype(BF16)
    pair_copy.start()
    relay(12)

    def o_step(group):
        for n in group:
            o_send[n] = partial(1, n).astype(BF16)
        for n in group:
            o_copy(n).start()

    o_step(range(parts // 2))
    q_step(second)
    p_step(third)
    pl.when(jnp.logical_not(early))(near_blocks)
    relay(10)
    q_step(third)
    o_step(range(parts // 2, parts))
    relay(11)
    pair_copy.wait_recv()
    pair_hop.start()
    h = low_of(xa, 0) + low_of(xa, 1)
    forward(xa, 2, ua)
    h = h + low_of(xa, 2)
    pair_hop.wait_recv()
    lg[...] = (pair[...].astype(F32) + pair_in[...].astype(F32)).astype(BF16)
    dd = remote(lg, lg_in, dp_s.at[1], dp_r.at[1], dp=1 - d)
    dd.start()
    all_f(xa, 0).wait_recv()
    forward(xa, 3, ua)
    h = h + low_of(xa, 3)
    ha[...] = h.astype(BF16)

    def out_body(n, carry):
        at = pl.ds(pl.multiple_of(n * tile, tile), tile)
        value, unused = gelu_pair(ua[n] + dot_nn(ha[...], upv[:, at]))
        base = xa[0, :, :, at].reshape(rows, tile).astype(F32)
        out_f[:, at] = (base + value).astype(BF16)
        return carry
    lax.fori_loop(0, tiles, out_body, 0)
    keeps = [
        pltpu.make_async_copy(out_f, keep_f, keep_sem.at[0]),
        pltpu.make_async_copy(out_u, keep_u, keep_sem.at[1]),
        pltpu.make_async_copy(out_d, keep_d, keep_sem.at[2]),
    ]
    keeps[0].start()

    for n in range(parts):
        own[n] = partial(0, n) + dot_nt(lg[...], dn[0, pl.ds(n * part, part), :])

    du.wait_recv()
    out_u[...] = (du_send[...].astype(F32) + du_recv[...].astype(F32)).astype(BF16)
    keeps[1].start()

    all_x.wait_recv()
    dd.wait_recv()
    here = dot_tn(lg[...], xb[0].reshape(rows, cols))
    there = dot_tn(lg_in[...], xo[...].reshape(rows, cols))
    out_d[...] = (here + there).T.astype(BF16)
    keeps[2].start()

    remote(o_send, o_recv, pqo_s.at[0], o_r.at[0], tensor=t1).wait_recv()
    for n in range(parts):
        q_copy(n).wait_recv()
        at = pl.ds(n * part, part)
        total = own[n] + o_recv[n].astype(F32) + q_recv[n].astype(F32)
        out_b[:, at] = (g[:, :, at].reshape(rows, part).astype(F32) + total).astype(BF16)
        pltpu.make_async_copy(out_b.at[:, at], keep_b.at[:, at], keep_sem.at[3]).start()

    def drain(v):
        for k in range(S):
            if k != v and ("w", ("b", k)) not in relay_slot(v, S, 0):
                ex(v, k).wait_send()
        if v < S - 1:
            remote(sent.at[1], xa.at[0], az_s.at[0], az_r.at[0], section=v + 1).wait_send()
        if v > 0:
            gz.wait_send()
    per_section(drain)
    all_x.wait_send()
    remote(xab.at[:, 0:3], xab.at[:, 1:4], hop_s.at[0], y_r.at[0], tensor=t1).wait_send()
    low_copy.wait_send()
    pair_copy.wait_send()
    pair_hop.wait_send()
    remote(pqo_send, pqo_send, pqo_s.at[0], p_r.at[0], tensor=t1).wait_send()
    du.wait_send()
    dd.wait_send()
    for keep in keeps:
        keep.wait()
    pltpu.make_async_copy(out_b, keep_b, keep_sem.at[3]).wait()


def store_kernel(*refs):
    copies = [pltpu.make_async_copy(refs[i], refs[4 + i], refs[8].at[i]) for i in range(4)]
    for copy in copies:
        copy.start()
    for copy in copies:
        copy.wait()


def fused_on_device(sent, stash, table, embedded, loss, weight, down, up):
    S = lax.axis_size("section")
    piece, cols = stash.shape[1], stash.shape[2]
    rows, rank = S * piece, up.shape[1]
    tile = next(k for k in (768, 512, 256, 128) if cols % k == 0)
    part = next(k for k in (384, 256, 128) if cols % k == 0)
    tiles, parts = cols // tile, cols // part
    far = lambda x: pltpu.with_memory_space_constraint(x, pltpu.HBM)
    hbm = pl.BlockSpec(memory_space=pltpu.HBM)
    smem = pl.BlockSpec(memory_space=pltpu.SMEM)
    V = pltpu.VMEM
    dma = lambda *shape: pltpu.SemaphoreType.DMA(shape)
    block = (tiles, rows, tile)
    cut = (parts, rows, part)
    slim = V((rows, rank), BF16)
    stack = V((S, piece, cols), BF16)
    outs = pl.pallas_call(
        functools.partial(window_kernel, S, tile, part),
        out_shape=(
            jax.ShapeDtypeStruct((rows, cols), BF16),
            jax.ShapeDtypeStruct((rows, cols), BF16),
            jax.ShapeDtypeStruct((cols, rank), BF16),
            jax.ShapeDtypeStruct((rank, cols), BF16),
        ),
        in_specs=[hbm, hbm, smem, hbm, hbm, hbm, hbm, hbm],
        out_specs=(pl.BlockSpec(memory_space=pl.ANY),) * 4,
        scratch_shapes=[
            V((rows, cols), BF16), V((rows, cols), BF16), V((cols, rank), BF16), V((rank, cols), BF16),
            stack, V((4, cols, cols), BF16), V((4, cols, rank), BF16), V((rank, cols), BF16),
            V((2, 4, S, piece, cols), BF16),
            stack, stack,
            V(block, F32), V(block, F32), V((rows, cols), BF16),
            slim, slim, slim, slim, slim, slim, slim, slim,
            V((3,) + cut, BF16), V(cut, BF16), V(cut, BF16), V(cut, BF16), V(cut, F32),
            V((rank, cols), BF16), V((rank, cols), BF16), stack,
            dma(4), dma(1), dma(4), dma(4), dma(S), dma(S), dma(1), dma(S), dma(1), dma(1),
            dma(1), dma(1), dma(1), dma(2 * S), dma(2), dma(2), dma(3), dma(3), dma(1), dma(3), dma(parts), dma(1),
            dma(2), dma(2),
        ],
        compiler_params=pltpu.CompilerParams(
            collective_id=0, has_side_effects=True, vmem_limit_bytes=44 * 1024 * 1024),
    )(
        far(sent.reshape(2, S, piece, cols)), far(stash), far(table),
        far(embedded.reshape(S, piece, cols)), far(loss.reshape(S, piece, cols)),
        far(weight.reshape(4, cols, cols)), far(down.reshape(4, cols, rank)), far(up[0]),
    )
    stored = pl.pallas_call(
        store_kernel,
        out_shape=tuple(jax.ShapeDtypeStruct(o.shape, o.dtype) for o in outs),
        in_specs=[pl.BlockSpec(memory_space=pl.ANY)] * 4,
        out_specs=(hbm,) * 4,
        scratch_shapes=[dma(4)],
        compiler_params=pltpu.CompilerParams(vmem_limit_bytes=1024 * 1024),
    )(*outs)
    return tuple(o[None] for o in stored)


def solution(mesh):
    placed = (
        P("section", "dp", "tensor"),
        P("section", "dp", "tensor"),
        P("section", None),
        P("dp", "tensor"),
        P("dp", "tensor"),
        P("section", None, "tensor"),
        P("section", None, None),
        P("section", None, "tensor"),
    )
    def program(*args):
        rows = args[1].shape[1] // mesh.shape["dp"]
        cols = args[1].shape[2] // mesh.shape["tensor"]
        fits = (
            mesh.shape["tensor"] == 4 and mesh.shape["dp"] == 2
            and rows % 16 == 0 and cols % 128 == 0
        )
        return sharded(fused_on_device if fits else on_device)(*args)

    def sharded(body):
      return jax.shard_map(
        body,
        mesh=mesh,
        in_specs=placed,
        out_specs=(
            P("section", "dp", "tensor"),
            P("section", "dp", "tensor"),
            P("section", "tensor", None),
            P("section", None, "tensor"),
        ),
        check_vma=False,
    )

    return program
```

```python
import functools

import jax
import jax.numpy as jnp
from jax import lax
from jax.experimental import pallas as pl
from jax.experimental.pallas import tpu as pltpu
from jax.sharding import PartitionSpec as P

coef = 0.7978845608028654


def shifted(block, axis, distance):
    devices = range(lax.axis_size(axis))
    route = [(i - distance, i) for i in devices if i - distance in devices]
    return lax.ppermute(block, axis, route)


def gelu_pair(u):
    inner = coef * (u + 0.044715 * u * u * u)
    tanh_v = jnp.tanh(inner)
    value = 0.5 * u * (1.0 + tanh_v)
    slope = 0.5 * (1.0 + tanh_v) + 0.5 * u * (1.0 - tanh_v * tanh_v) * coef * (
        1.0 + 3.0 * 0.044715 * u * u
    )
    return (value, slope)


def on_device(
    sent,
    stashed_inputs,
    table,
    embedded,
    loss_gradient,
    weight,
    adapter_down_weight,
    adapter_up_weight,
):
    section = lax.axis_index("section")
    sections = lax.axis_size("section")
    w_section = weight[0]
    down_matrix = adapter_down_weight[0]
    up_matrix = adapter_up_weight[0]
    below = shifted(sent[1], "section", 1)
    above = shifted(sent[0], "section", -1)
    forward_input = jnp.where(section == 0, embedded, below)
    incoming_gradient = jnp.where(section == sections - 1, loss_gradient, above)
    order = jnp.argsort(table[0])
    arranged = jnp.take(stashed_inputs, order, axis=0)
    fetched = lax.all_to_all(arranged, "section", split_axis=0, concat_axis=0, tiled=True)
    backward_input = fetched.reshape(-1, fetched.shape[-1])
    full_a, full_b = (
        lax.all_gather(forward_input, "tensor", axis=1, tiled=True),
        lax.all_gather(backward_input, "tensor", axis=1, tiled=True),
    )
    main_a = jnp.dot(full_a, w_section, preferred_element_type=jnp.float32)
    h_a = jnp.dot(full_a, down_matrix, preferred_element_type=jnp.float32).astype(jnp.bfloat16)
    u_a = main_a + jnp.dot(h_a, up_matrix, preferred_element_type=jnp.float32)
    value_a, unused = gelu_pair(u_a)
    forward_output = (forward_input.astype(jnp.float32) + value_a).astype(jnp.bfloat16)
    h_b = jnp.dot(full_b, down_matrix, preferred_element_type=jnp.float32).astype(jnp.bfloat16)
    u_b = jnp.dot(full_b, w_section, preferred_element_type=jnp.float32) + jnp.dot(
        h_b, up_matrix, preferred_element_type=jnp.float32
    )
    unused_b, slope_b = gelu_pair(u_b)
    scaled = (incoming_gradient.astype(jnp.float32) * slope_b).astype(jnp.bfloat16)
    low_part = lax.dot_general(
        scaled, up_matrix, (((1,), (1,)), ((), ())), preferred_element_type=jnp.float32
    )
    low_piece = low_part.astype(jnp.bfloat16)
    partial_value = lax.dot_general(
        scaled, w_section, (((1,), (1,)), ((), ())), preferred_element_type=jnp.float32
    )
    partial_value = partial_value + lax.dot_general(
        low_piece, down_matrix, (((1,), (1,)), ((), ())), preferred_element_type=jnp.float32
    )
    input_grad = lax.psum_scatter(
        partial_value.astype(jnp.bfloat16), "tensor", scatter_dimension=1, tiled=True
    ).astype(jnp.float32)
    backward_output = (incoming_gradient.astype(jnp.float32) + input_grad).astype(jnp.bfloat16)
    low_grad = lax.psum(low_part.astype(jnp.bfloat16), "tensor")
    down_term = lax.dot_general(
        backward_input, low_grad, (((0,), (0,)), ((), ())), preferred_element_type=jnp.float32
    )
    up_term = lax.dot_general(
        h_b, scaled, (((0,), (0,)), ((), ())), preferred_element_type=jnp.float32
    )
    down_sum, up_sum = (
        lax.psum(down_term.astype(jnp.bfloat16), "dp").astype(jnp.float32),
        lax.psum(up_term.astype(jnp.bfloat16), "dp").astype(jnp.float32),
    )
    down_gradient = down_sum.astype(jnp.bfloat16)
    up_gradient = up_sum.astype(jnp.bfloat16)
    return (forward_output[None], backward_output[None], down_gradient[None], up_gradient[None])


F32 = jnp.float32
BF16 = jnp.bfloat16
MESH = pl.DeviceIdType.MESH


def dot_nn(a, b):
    return lax.dot_general(a, b, (((1,), (0,)), ((), ())), preferred_element_type=F32)


def dot_nt(a, b):
    return lax.dot_general(a, b, (((1,), (1,)), ((), ())), preferred_element_type=F32)


def dot_tn(a, b):
    return lax.dot_general(a, b, (((0,), (0,)), ((), ())), preferred_element_type=F32)


def stash_order(s, S):
    return sorted(range(S), key=lambda k: (abs(k - s), k))


def link_order(s, S):
    return [("b", k) for k in stash_order(s, S)] + [("a", c) for c in range(S)]


FOUR = {
    0: {
        0: ("a0", "~b1", "+b2", "b0'", "b1", "~b2", "+b3", "+a0", "a0'", "b1'", "a1", "+a1", "b2", "+a2", "b3",),
        1: ("b2'", "+a3",),
        2: ("b3'", "a2",),
        3: ("a3",),
        9: ("a1'",),
        10: ("a2'", "a3'",),
    },
    1: {
        0: ("~b2", "+b3", "b0", "b1'", "b2", "+g", "+a0", "b0'", "b3",),
        1: ("+a1", "b2'", "a0",),
        2: ("+a2", "b3'",),
        3: ("a1", "+a3",),
        4: ("a2",),
        5: ("a0'", "a3",),
        6: ("a1'",),
        9: ("a2'",),
        10: ("a3'",),
    },
    2: {
        0: ("~b3", "+a0", "~b1", "+b0", "b3", "b2'", "b1", "+g", "b3'", "b0", "+a1",),
        1: ("b1'", "+a2",),
        2: ("b0'", "+a3", "a0",),
        4: ("a1",),
        5: ("a0'",),
        7: ("a2",),
        8: ("a3",),
        9: ("a1'",),
        10: ("a2'",),
        11: ("a3'",),
    },
    3: {
        0: ("~b2", "+b1", "b3'", "b2", "+b0", "+g", "a0", "b2'", "b1", "a0'", "b0",),
        1: ("b1'",),
        2: ("b0'", "a1",),
        3: ("a2",),
        5: ("a3",),
        9: ("a1'",),
        10: ("a2'",),
        11: ("a3'",),
    },
}


def read_plan(words):
    plan = []
    for word in words:
        kind = "s" if word[0] == "+" else "w" if word[0] == "~" else "q" if word[-1] == "'" else "p"
        name = word.strip("+~'")
        plan.append((kind, (name[0], int(name[1:] or 0))))
    return plan


def first_targets(s, S):
    order = stash_order(s, S)[1:]
    held = [item[1] for kind, item in relay_slot(s, S, 0) if kind == "s" and item[0] == "b"]
    return [k for k in order if k not in held]


def relay_slot(s, S, slot):
    if S == 4:
        return read_plan(FOUR[s].get(slot, ()))
    order = link_order(s, S)[1:]
    if slot == 0:
        late = [("s", ("a", c)) for c in range(S) if s < S - 1] + [("s", ("g", 0))] * (s > 0)
        return [("p", item) for item in order if item[0] == "b"] + late
    if slot == 2:
        return [("q", ("b", k)) for k in range(S)]
    if slot == 5:
        return [(kind, item) for item in order if item[0] == "a" for kind in "pq"]
    return []


def window_kernel(
    sections, tile, part,
    sent, stash_hbm, table_hbm, embedded, loss, weight, down, up,
    keep_f, keep_b, keep_d, keep_u,
    out_f, out_b, out_d, out_u,
    table, stash_v, w, dn, upv, xab, g, arranged, u, ua, scaled, low, low_in, pair, pair_in, lg, lg_in, hb, ha,
    pqo_send, p_recv, q_recv, o_recv, own,
    du_send, du_recv, xo,
    w_sem, d_sem, loc_sem, keep_sem, ex_s, ex_r, az_s, az_r, gz_s, gz_r,
    xo_s, xo_r, hop_s, y_r, c_r, f_r, low_s, low_r, pqo_s, p_r, q_r, o_r, dp_s, dp_r,
):
    S = sections
    xa, xb = xab.at[0], xab.at[1]
    p_send, q_send, o_send = pqo_send.at[0], pqo_send.at[1], pqo_send.at[2]
    s = lax.axis_index("section")
    d = lax.axis_index("dp")
    t = lax.axis_index("tensor")
    t1 = t + 1 - 2 * (t % 2)
    t2 = (t + 2) % 4
    t3 = (t1 + 2) % 4
    rel = [t, t1, t2, t3]
    piece, cols = stash_v.shape[1], stash_v.shape[2]
    rows = S * piece
    tiles = cols // tile
    parts = cols // part
    stash_copy = pltpu.make_async_copy(stash_hbm, stash_v, loc_sem.at[0])
    stash_copy.start()
    table_copy = pltpu.make_async_copy(table_hbm, table, loc_sem.at[4])
    table_copy.start()

    def remote(src, dst, ss, rs, **device):
        return pltpu.make_async_remote_copy(
            src_ref=src, dst_ref=dst, send_sem=ss, recv_sem=rs,
            device_id=device, device_id_type=MESH)

    emb_copy = pltpu.make_async_copy(embedded, xa.at[0], loc_sem.at[3])
    loss_copy = pltpu.make_async_copy(loss, g, loc_sem.at[1])
    up_copy = pltpu.make_async_copy(up, upv, loc_sem.at[2])
    w_copies = [pltpu.make_async_copy(weight.at[rel[r]], w.at[r], w_sem.at[r]) for r in range(4)]
    d_copies = [pltpu.make_async_copy(down.at[rel[r]], dn.at[r], d_sem.at[0]) for r in range(4)]
    d_all = pltpu.make_async_copy(down, dn, d_sem.at[0])

    barrier = pltpu.get_barrier_semaphore()
    for j in range(1, S):
        pl.semaphore_signal(barrier, inc=1, device_id={"section": (s + j) % S}, device_id_type=MESH)
    for r in range(1, 4):
        pl.semaphore_signal(barrier, inc=1, device_id={"tensor": rel[r]}, device_id_type=MESH)
    pl.semaphore_signal(barrier, inc=1, device_id={"dp": 1 - d}, device_id_type=MESH)

    @pl.when(s == 0)
    def _():
        emb_copy.start()

    table_copy.wait()
    stash_copy.wait()
    for j in range(S):
        dest = (s + j) % S
        k = jnp.int32(0)
        for i in range(S):
            k = jnp.where(table[0, i] == dest, i, k)
        if j == 0:
            xb[0, s] = stash_v[k]
        else:
            arranged[j] = stash_v[k]
    pl.semaphore_wait(barrier, S + 3)

    def ex(v, to):
        return remote(arranged.at[(to - v) % S], xb.at[0, v], ex_s.at[to], ex_r.at[v], section=to)

    def az(v, c):
        return remote(sent.at[1, c], xa.at[0, c], az_s.at[0], az_r.at[c], section=(v + 1) % S)

    gz = remote(sent.at[0], g, gz_s.at[0], gz_r.at[0], section=(s + S - 1) % S)

    def place(item):
        kind = 1 if item[0] == "b" else 0
        return (xb if kind else xa), item[1], kind

    def hop_y(item):
        x, k, kind = place(item)
        return remote(x.at[0, k], x.at[2, k], hop_s.at[0], y_r.at[kind * S + k], tensor=t2)

    def hop_c(item):
        x, k, kind = place(item)
        return remote(x.at[0, k], x.at[1, k], hop_s.at[0], c_r.at[kind], tensor=t1)

    def hop_f(item):
        x, k, kind = place(item)
        return remote(x.at[2, k], x.at[3, k], hop_s.at[0], f_r.at[kind], tensor=t1)

    def all_c(x, kind):
        return remote(x.at[0], x.at[1], hop_s.at[0], c_r.at[kind], tensor=t1)

    def all_f(x, kind):
        return remote(x.at[2], x.at[3], hop_s.at[0], f_r.at[kind], tensor=t1)

    def hop_x(k):
        return remote(xb.at[0, k], xo.at[k], xo_s.at[0], xo_r.at[0], dp=1 - d)

    all_x = remote(xb.at[0], xo, xo_s.at[0], xo_r.at[0], dp=1 - d)

    def act(v, step):
        kind, item = step
        if kind in "sw":
            copy = gz if item[0] == "g" else az(v, item[1]) if item[0] == "a" else ex(v, item[1])
            copy.start() if kind == "s" else copy.wait_send()
            return
        if kind == "q":
            hop_y(item).wait_recv()
            hop_f(item).start()
            return
        if item[0] == "b":
            if item[1] != v:
                ex(item[1], v).wait_recv()
        elif v == 0:
            if item[1] == 0:
                emb_copy.wait()
        else:
            az(v - 1, item[1]).wait_recv()
        hop_y(item).start()
        hop_c(item).start()
        if item[0] == "b":
            hop_x(item[1]).start()

    def per_section(run):
        for v in range(S):
            pl.when(s == v)(functools.partial(run, v))

    def relay(slot):
        def run(v):
            for step in relay_slot(v, S, slot):
                act(v, step)
        per_section(run)

    def first_sends(v):
        act(v, ("p", ("b", v)))
        for k in first_targets(v, S):
            ex(v, k).start()
        if v == S - 1:
            loss_copy.start()
    per_section(first_sends)

    for r in range(4):
        d_copies[r].start()
        w_copies[r].start()
    up_copy.start()

    def run_rest(v):
        for step in relay_slot(v, S, 0):
            act(v, step)
    per_section(run_rest)

    def forward(x, r, acc):
        for n in range(tiles):
            val = dot_nn(x[r].reshape(rows, cols), w[r, :, pl.ds(n * tile, tile)])
            acc[n] = val if r == 0 else acc[n] + val

    def low_of(x, r):
        return dot_nn(x[r].reshape(rows, cols), dn[r])

    d_all.wait()
    w_copies[0].wait()
    forward(xb, 0, u)
    h = low_of(xb, 0)
    relay(1)
    all_c(xb, 1).wait_recv()
    w_copies[1].wait()
    forward(xb, 1, u)
    h = h + low_of(xb, 1)
    relay(2)
    w_copies[2].wait()
    forward(xb, 2, u)
    h = h + low_of(xb, 2)
    relay(3)
    all_f(xb, 1).wait_recv()
    w_copies[3].wait()
    forward(xb, 3, u)
    h = h + low_of(xb, 3)
    hb[...] = h.astype(BF16)
    relay(4)
    up_copy.wait()

    def slope_body(n, carry):
        at = pl.ds(pl.multiple_of(n * tile, tile), tile)
        unused, slope = gelu_pair(u[n] + dot_nn(hb[...], upv[:, at]))
        u[n] = slope
        return carry
    lax.fori_loop(0, tiles, slope_body, 0)
    relay(5)
    relay(6)

    def near_blocks():
        forward(xa, 0, ua)
        all_c(xa, 0).wait_recv()
        forward(xa, 1, ua)
    early = (s > 0) & (s < S // 2)
    pl.when(early)(near_blocks)
    relay(7)

    @pl.when(s == S - 1)
    def _():
        loss_copy.wait()

    @pl.when(s < S - 1)
    def _():
        gz.wait_recv()

    def scale_body(n, carry):
        at = pl.ds(pl.multiple_of(n * tile, tile), tile)
        scaled[:, at] = (g[:, :, at].reshape(rows, tile).astype(F32) * u[n]).astype(BF16)
        return carry
    lax.fori_loop(0, tiles, scale_body, 0)

    low_copy = remote(low, low_in, low_s.at[0], low_r.at[0], tensor=t1)
    share = rows // 2
    lower = pl.ds(pl.multiple_of((t % 2) * share, share), share)
    pair_copy = remote(pair.at[lower], pair_in.at[lower], low_s.at[1], low_r.at[1], tensor=t2)
    pair_hop = remote(pair_in.at[lower], pair_in.at[lower], low_s.at[2], low_r.at[2], tensor=t1)

    def partial(r, n):
        return dot_nt(scaled[...], w[r, pl.ds(n * part, part), :])

    def p_copy(n):
        return remote(p_send.at[n], p_recv.at[n], pqo_s.at[0], p_r.at[(n >= lead) + (n >= parts - lead)], tensor=t1)

    def p_group(group):
        at = pl.ds(group[0], len(group))
        which = (group[0] >= lead) + (group[0] >= parts - lead)
        return remote(p_send.at[at], p_recv.at[at], pqo_s.at[0], p_r.at[which], tensor=t1)

    def q_copy(n):
        return remote(q_send.at[n], q_recv.at[n], pqo_s.at[0], q_r.at[n], tensor=t2)

    def o_copy(n):
        return remote(o_send.at[n], o_recv.at[n], pqo_s.at[0], o_r.at[0], tensor=t1)

    lead = max(parts // 4, 1)
    first, second, third = range(lead), range(lead, parts - lead), range(parts - lead, parts)

    def p_step(group):
        for n in group:
            p_send[n] = partial(3, n).astype(BF16)
        for n in group:
            p_copy(n).start()

    def q_step(group):
        for n in group:
            own[n] = partial(2, n)
        p_group(group).wait_recv()
        for n in group:
            q_send[n] = (own[n] + p_recv[n].astype(F32)).astype(BF16)
        for n in group:
            q_copy(n).start()

    p_step(first)
    low[...] = dot_nt(scaled[...], upv[...]).astype(BF16)
    low_copy.start()
    relay(8)
    q_step(first)
    relay(9)
    p_step(second)
    du_send[...] = dot_tn(hb[...], scaled[...]).astype(BF16)
    du = remote(du_send, du_recv, dp_s.at[0], dp_r.at[0], dp=1 - d)
    du.start()
    low_copy.wait_recv()
    pair[...] = (low[...].astype(F32) + low_in[...].astype(F32)).astype(BF16)
    pair_copy.start()
    relay(12)

    def o_step(group):
        for n in group:
            o_send[n] = partial(1, n).astype(BF16)
        for n in group:
            o_copy(n).start()

    o_step(range(parts // 2))
    q_step(second)
    p_step(third)
    pl.when(jnp.logical_not(early))(near_blocks)
    relay(10)
    q_step(third)
    o_step(range(parts // 2, parts))
    relay(11)
    pair_copy.wait_recv()
    pair_hop.start()
    h = low_of(xa, 0) + low_of(xa, 1)
    forward(xa, 2, ua)
    h = h + low_of(xa, 2)
    pair_hop.wait_recv()
    lg[...] = (pair[...].astype(F32) + pair_in[...].astype(F32)).astype(BF16)
    dd = remote(lg, lg_in, dp_s.at[1], dp_r.at[1], dp=1 - d)
    dd.start()
    all_f(xa, 0).wait_recv()
    forward(xa, 3, ua)
    h = h + low_of(xa, 3)
    ha[...] = h.astype(BF16)

    def out_body(n, carry):
        at = pl.ds(pl.multiple_of(n * tile, tile), tile)
        value, unused = gelu_pair(ua[n] + dot_nn(ha[...], upv[:, at]))
        base = xa[0, :, :, at].reshape(rows, tile).astype(F32)
        out_f[:, at] = (base + value).astype(BF16)
        return carry
    lax.fori_loop(0, tiles, out_body, 0)
    keeps = [
        pltpu.make_async_copy(out_f, keep_f, keep_sem.at[0]),
        pltpu.make_async_copy(out_u, keep_u, keep_sem.at[1]),
        pltpu.make_async_copy(out_d, keep_d, keep_sem.at[2]),
    ]
    keeps[0].start()

    for n in range(parts):
        own[n] = partial(0, n) + dot_nt(lg[...], dn[0, pl.ds(n * part, part), :])

    du.wait_recv()
    out_u[...] = (du_send[...].astype(F32) + du_recv[...].astype(F32)).astype(BF16)
    keeps[1].start()

    all_x.wait_recv()
    dd.wait_recv()
    here = dot_tn(lg[...], xb[0].reshape(rows, cols))
    there = dot_tn(lg_in[...], xo[...].reshape(rows, cols))
    out_d[...] = (here + there).T.astype(BF16)
    keeps[2].start()

    remote(o_send, o_recv, pqo_s.at[0], o_r.at[0], tensor=t1).wait_recv()
    for n in range(parts):
        q_copy(n).wait_recv()
        at = pl.ds(n * part, part)
        total = own[n] + o_recv[n].astype(F32) + q_recv[n].astype(F32)
        out_b[:, at] = (g[:, :, at].reshape(rows, part).astype(F32) + total).astype(BF16)
        pltpu.make_async_copy(out_b.at[:, at], keep_b.at[:, at], keep_sem.at[3]).start()

    def drain(v):
        for k in range(S):
            if k != v and ("w", ("b", k)) not in relay_slot(v, S, 0):
                ex(v, k).wait_send()
        if v < S - 1:
            remote(sent.at[1], xa.at[0], az_s.at[0], az_r.at[0], section=v + 1).wait_send()
        if v > 0:
            gz.wait_send()
    per_section(drain)
    all_x.wait_send()
    remote(xab.at[:, 0:3], xab.at[:, 1:4], hop_s.at[0], y_r.at[0], tensor=t1).wait_send()
    low_copy.wait_send()
    pair_copy.wait_send()
    pair_hop.wait_send()
    remote(pqo_send, pqo_send, pqo_s.at[0], p_r.at[0], tensor=t1).wait_send()
    du.wait_send()
    dd.wait_send()
    for keep in keeps:
        keep.wait()
    pltpu.make_async_copy(out_b, keep_b, keep_sem.at[3]).wait()


def store_kernel(*refs):
    copies = [pltpu.make_async_copy(refs[i], refs[4 + i], refs[8].at[i]) for i in range(4)]
    for copy in copies:
        copy.start()
    for copy in copies:
        copy.wait()


def fused_on_device(sent, stash, table, embedded, loss, weight, down, up):
    S = lax.axis_size("section")
    piece, cols = stash.shape[1], stash.shape[2]
    rows, rank = S * piece, up.shape[1]
    tile = next(k for k in (768, 512, 256, 128) if cols % k == 0)
    part = next(k for k in (384, 256, 128) if cols % k == 0)
    tiles, parts = cols // tile, cols // part
    far = lambda x: pltpu.with_memory_space_constraint(x, pltpu.HBM)
    hbm = pl.BlockSpec(memory_space=pltpu.HBM)
    V = pltpu.VMEM
    dma = lambda *shape: pltpu.SemaphoreType.DMA(shape)
    block = (tiles, rows, tile)
    cut = (parts, rows, part)
    slim = V((rows, rank), BF16)
    stack = V((S, piece, cols), BF16)
    outs = pl.pallas_call(
        functools.partial(window_kernel, S, tile, part),
        out_shape=(
            jax.ShapeDtypeStruct((rows, cols), BF16),
            jax.ShapeDtypeStruct((rows, cols), BF16),
            jax.ShapeDtypeStruct((cols, rank), BF16),
            jax.ShapeDtypeStruct((rank, cols), BF16),
        ),
        in_specs=[hbm, hbm, hbm, hbm, hbm, hbm, hbm, hbm],
        out_specs=(pl.BlockSpec(memory_space=pl.ANY),) * 4,
        scratch_shapes=[
            V((rows, cols), BF16), V((rows, cols), BF16), V((cols, rank), BF16), V((rank, cols), BF16),
            pltpu.SMEM(table.shape, table.dtype), stack, V((4, cols, cols), BF16), V((4, cols, rank), BF16), V((rank, cols), BF16),
            V((2, 4, S, piece, cols), BF16),
            stack, stack,
            V(block, F32), V(block, F32), V((rows, cols), BF16),
            slim, slim, slim, slim, slim, slim, slim, slim,
            V((3,) + cut, BF16), V(cut, BF16), V(cut, BF16), V(cut, BF16), V(cut, F32),
            V((rank, cols), BF16), V((rank, cols), BF16), stack,
            dma(4), dma(1), dma(5), dma(4), dma(S), dma(S), dma(1), dma(S), dma(1), dma(1),
            dma(1), dma(1), dma(1), dma(2 * S), dma(2), dma(2), dma(3), dma(3), dma(1), dma(3), dma(parts), dma(1),
            dma(2), dma(2),
        ],
        compiler_params=pltpu.CompilerParams(
            collective_id=0, has_side_effects=True, vmem_limit_bytes=44 * 1024 * 1024),
    )(
        far(sent.reshape(2, S, piece, cols)), far(stash), far(table),
        far(embedded.reshape(S, piece, cols)), far(loss.reshape(S, piece, cols)),
        far(weight.reshape(4, cols, cols)), far(down.reshape(4, cols, rank)), far(up[0]),
    )
    stored = pl.pallas_call(
        store_kernel,
        out_shape=tuple(jax.ShapeDtypeStruct(o.shape, o.dtype) for o in outs),
        in_specs=[pl.BlockSpec(memory_space=pl.ANY)] * 4,
        out_specs=(hbm,) * 4,
        scratch_shapes=[dma(4)],
        compiler_params=pltpu.CompilerParams(vmem_limit_bytes=1024 * 1024),
    )(*outs)
    return tuple(o[None] for o in stored)


def solution(mesh):
    placed = (
        P("section", "dp", "tensor"),
        P("section", "dp", "tensor"),
        P("section", None),
        P("dp", "tensor"),
        P("dp", "tensor"),
        P("section", None, "tensor"),
        P("section", None, None),
        P("section", None, "tensor"),
    )
    def program(*args):
        rows = args[1].shape[1] // mesh.shape["dp"]
        cols = args[1].shape[2] // mesh.shape["tensor"]
        fits = (
            mesh.shape["tensor"] == 4 and mesh.shape["dp"] == 2
            and rows % 16 == 0 and cols % 128 == 0
        )
        return sharded(fused_on_device if fits else on_device)(*args)

    def sharded(body):
      return jax.shard_map(
        body,
        mesh=mesh,
        in_specs=placed,
        out_specs=(
            P("section", "dp", "tensor"),
            P("section", "dp", "tensor"),
            P("section", "tensor", None),
            P("section", None, "tensor"),
        ),
        check_vma=False,
    )

    return program
```

```python
import functools

import jax
import jax.numpy as jnp
from jax import lax
from jax.experimental import pallas as pl
from jax.experimental.pallas import tpu as pltpu
from jax.sharding import PartitionSpec as P

coef = 0.7978845608028654


def shifted(block, axis, distance):
    devices = range(lax.axis_size(axis))
    route = [(i - distance, i) for i in devices if i - distance in devices]
    return lax.ppermute(block, axis, route)


def gelu_pair(u):
    inner = coef * (u + 0.044715 * u * u * u)
    tanh_v = jnp.tanh(inner)
    value = 0.5 * u * (1.0 + tanh_v)
    slope = 0.5 * (1.0 + tanh_v) + 0.5 * u * (1.0 - tanh_v * tanh_v) * coef * (
        1.0 + 3.0 * 0.044715 * u * u
    )
    return (value, slope)


def on_device(
    sent,
    stashed_inputs,
    table,
    embedded,
    loss_gradient,
    weight,
    adapter_down_weight,
    adapter_up_weight,
):
    section = lax.axis_index("section")
    sections = lax.axis_size("section")
    w_section = weight[0]
    down_matrix = adapter_down_weight[0]
    up_matrix = adapter_up_weight[0]
    below = shifted(sent[1], "section", 1)
    above = shifted(sent[0], "section", -1)
    forward_input = jnp.where(section == 0, embedded, below)
    incoming_gradient = jnp.where(section == sections - 1, loss_gradient, above)
    order = jnp.argsort(table[0])
    arranged = jnp.take(stashed_inputs, order, axis=0)
    fetched = lax.all_to_all(arranged, "section", split_axis=0, concat_axis=0, tiled=True)
    backward_input = fetched.reshape(-1, fetched.shape[-1])
    full_a, full_b = (
        lax.all_gather(forward_input, "tensor", axis=1, tiled=True),
        lax.all_gather(backward_input, "tensor", axis=1, tiled=True),
    )
    main_a = jnp.dot(full_a, w_section, preferred_element_type=jnp.float32)
    h_a = jnp.dot(full_a, down_matrix, preferred_element_type=jnp.float32).astype(jnp.bfloat16)
    u_a = main_a + jnp.dot(h_a, up_matrix, preferred_element_type=jnp.float32)
    value_a, unused = gelu_pair(u_a)
    forward_output = (forward_input.astype(jnp.float32) + value_a).astype(jnp.bfloat16)
    h_b = jnp.dot(full_b, down_matrix, preferred_element_type=jnp.float32).astype(jnp.bfloat16)
    u_b = jnp.dot(full_b, w_section, preferred_element_type=jnp.float32) + jnp.dot(
        h_b, up_matrix, preferred_element_type=jnp.float32
    )
    unused_b, slope_b = gelu_pair(u_b)
    scaled = (incoming_gradient.astype(jnp.float32) * slope_b).astype(jnp.bfloat16)
    low_part = lax.dot_general(
        scaled, up_matrix, (((1,), (1,)), ((), ())), preferred_element_type=jnp.float32
    )
    low_piece = low_part.astype(jnp.bfloat16)
    partial_value = lax.dot_general(
        scaled, w_section, (((1,), (1,)), ((), ())), preferred_element_type=jnp.float32
    )
    partial_value = partial_value + lax.dot_general(
        low_piece, down_matrix, (((1,), (1,)), ((), ())), preferred_element_type=jnp.float32
    )
    input_grad = lax.psum_scatter(
        partial_value.astype(jnp.bfloat16), "tensor", scatter_dimension=1, tiled=True
    ).astype(jnp.float32)
    backward_output = (incoming_gradient.astype(jnp.float32) + input_grad).astype(jnp.bfloat16)
    low_grad = lax.psum(low_part.astype(jnp.bfloat16), "tensor")
    down_term = lax.dot_general(
        backward_input, low_grad, (((0,), (0,)), ((), ())), preferred_element_type=jnp.float32
    )
    up_term = lax.dot_general(
        h_b, scaled, (((0,), (0,)), ((), ())), preferred_element_type=jnp.float32
    )
    down_sum, up_sum = (
        lax.psum(down_term.astype(jnp.bfloat16), "dp").astype(jnp.float32),
        lax.psum(up_term.astype(jnp.bfloat16), "dp").astype(jnp.float32),
    )
    down_gradient = down_sum.astype(jnp.bfloat16)
    up_gradient = up_sum.astype(jnp.bfloat16)
    return (forward_output[None], backward_output[None], down_gradient[None], up_gradient[None])


F32 = jnp.float32
BF16 = jnp.bfloat16
MESH = pl.DeviceIdType.MESH


def dot_nn(a, b):
    return lax.dot_general(a, b, (((1,), (0,)), ((), ())), preferred_element_type=F32)


def dot_nt(a, b):
    return lax.dot_general(a, b, (((1,), (1,)), ((), ())), preferred_element_type=F32)


def dot_tn(a, b):
    return lax.dot_general(a, b, (((0,), (0,)), ((), ())), preferred_element_type=F32)


def stash_order(s, S):
    return sorted(range(S), key=lambda k: (abs(k - s), k))


def link_order(s, S):
    return [("b", k) for k in stash_order(s, S)] + [("a", c) for c in range(S)]


FOUR = {
    0: {
        0: ("a0", "~b1", "+b2", "b0'", "b1", "~b2", "+b3", "+a0", "a0'", "b1'", "a1", "+a1", "b2", "+a2", "b3",),
        1: ("b2'", "+a3",),
        2: ("b3'", "a2",),
        3: ("a3",),
        9: ("a1'",),
        10: ("a2'", "a3'",),
    },
    1: {
        0: ("~b2", "+b3", "b0", "b1'", "b2", "+g", "+a0", "b0'", "b3",),
        1: ("+a1", "b2'", "a0",),
        2: ("+a2", "b3'",),
        3: ("a1", "+a3",),
        4: ("a2",),
        5: ("a0'", "a3",),
        6: ("a1'",),
        9: ("a2'",),
        10: ("a3'",),
    },
    2: {
        0: ("~b3", "+a0", "~b1", "+b0", "b3", "b2'", "b1", "+g", "b3'", "b0", "+a1",),
        1: ("b1'", "+a2",),
        2: ("b0'", "+a3", "a0",),
        4: ("a1",),
        5: ("a0'",),
        7: ("a2",),
        8: ("a3",),
        9: ("a1'",),
        10: ("a2'",),
        11: ("a3'",),
    },
    3: {
        0: ("~b2", "+b1", "b3'", "b2", "+b0", "+g", "a0", "b2'", "b1", "a0'", "b0",),
        1: ("b1'",),
        2: ("b0'", "a1",),
        3: ("a2",),
        5: ("a3",),
        9: ("a1'",),
        10: ("a2'",),
        11: ("a3'",),
    },
}


def read_plan(words):
    plan = []
    for word in words:
        kind = "s" if word[0] == "+" else "w" if word[0] == "~" else "q" if word[-1] == "'" else "p"
        name = word.strip("+~'")
        plan.append((kind, (name[0], int(name[1:] or 0))))
    return plan


def first_targets(s, S):
    order = stash_order(s, S)[1:]
    held = [item[1] for kind, item in relay_slot(s, S, 0) if kind == "s" and item[0] == "b"]
    return [k for k in order if k not in held]


def relay_slot(s, S, slot):
    if S == 4:
        return read_plan(FOUR[s].get(slot, ()))
    order = link_order(s, S)[1:]
    if slot == 0:
        late = [("s", ("a", c)) for c in range(S) if s < S - 1] + [("s", ("g", 0))] * (s > 0)
        return [("p", item) for item in order if item[0] == "b"] + late
    if slot == 2:
        return [("q", ("b", k)) for k in range(S)]
    if slot == 5:
        return [(kind, item) for item in order if item[0] == "a" for kind in "pq"]
    return []


def window_kernel(
    sections, tile, part,
    sent, stash_hbm, table_hbm, embedded, loss, weight, down, up,
    keep_f, keep_b, keep_d, keep_u,
    out_f, out_b, out_d, out_u,
    table, stash_v, w, dn, upv, xab, g, arranged, u, ua, scaled, low, low_in, pair, pair_in, lg, lg_in, hb, ha,
    pqo_send, p_recv, q_recv, o_recv, own,
    du_send, du_recv, xo,
    w_sem, d_sem, loc_sem, keep_sem, ex_s, ex_r, az_s, az_r, gz_s, gz_r,
    xo_s, xo_r, hop_s, y_r, c_r, f_r, low_s, low_r, pqo_s, p_r, q_r, o_r, dp_s, dp_r,
):
    S = sections
    xa, xb = xab.at[0], xab.at[1]
    p_send, q_send, o_send = pqo_send.at[0], pqo_send.at[1], pqo_send.at[2]
    s = lax.axis_index("section")
    d = lax.axis_index("dp")
    t = lax.axis_index("tensor")
    t1 = t + 1 - 2 * (t % 2)
    t2 = (t + 2) % 4
    t3 = (t1 + 2) % 4
    rel = [t, t1, t2, t3]
    piece, cols = stash_v.shape[1], stash_v.shape[2]
    rows = S * piece
    tiles = cols // tile
    parts = cols // part
    stash_copy = pltpu.make_async_copy(stash_hbm, stash_v, loc_sem.at[0])
    stash_copy.start()
    table_copy = pltpu.make_async_copy(table_hbm, table, loc_sem.at[4])
    table_copy.start()

    def remote(src, dst, ss, rs, **device):
        return pltpu.make_async_remote_copy(
            src_ref=src, dst_ref=dst, send_sem=ss, recv_sem=rs,
            device_id=device, device_id_type=MESH)

    emb_copy = pltpu.make_async_copy(embedded, xa.at[0], loc_sem.at[3])
    loss_copy = pltpu.make_async_copy(loss, g, loc_sem.at[1])
    up_copy = pltpu.make_async_copy(up, upv, loc_sem.at[2])
    w_copies = [pltpu.make_async_copy(weight.at[rel[r]], w.at[r], w_sem.at[r]) for r in range(4)]
    d_copies = [pltpu.make_async_copy(down.at[rel[r]], dn.at[r], d_sem.at[0]) for r in range(4)]
    d_all = pltpu.make_async_copy(down, dn, d_sem.at[0])

    barrier = pltpu.get_barrier_semaphore()
    for j in range(1, S):
        pl.semaphore_signal(barrier, inc=1, device_id={"section": (s + j) % S}, device_id_type=MESH)
    for r in range(1, 4):
        pl.semaphore_signal(barrier, inc=1, device_id={"tensor": rel[r]}, device_id_type=MESH)
    pl.semaphore_signal(barrier, inc=1, device_id={"dp": 1 - d}, device_id_type=MESH)

    @pl.when(s == 0)
    def _():
        emb_copy.start()

    table_copy.wait()
    stash_copy.wait()
    for j in range(S):
        dest = (s + j) % S
        k = jnp.int32(0)
        for i in range(S):
            k = jnp.where(table[0, i] == dest, i, k)
        if j == 0:
            xb[0, s] = stash_v[k]
        else:
            arranged[j] = stash_v[k]
    pl.semaphore_wait(barrier, S + 3)

    def ex(v, to):
        return remote(arranged.at[(to - v) % S], xb.at[0, v], ex_s.at[to], ex_r.at[v], section=to)

    def az(v, c):
        return remote(sent.at[1, c], xa.at[0, c], az_s.at[0], az_r.at[c], section=(v + 1) % S)

    gz = remote(sent.at[0], g, gz_s.at[0], gz_r.at[0], section=(s + S - 1) % S)

    def place(item):
        kind = 1 if item[0] == "b" else 0
        return (xb if kind else xa), item[1], kind

    def hop_y(item):
        x, k, kind = place(item)
        return remote(x.at[0, k], x.at[2, k], hop_s.at[0], y_r.at[kind * S + k], tensor=t2)

    def hop_c(item):
        x, k, kind = place(item)
        return remote(x.at[0, k], x.at[1, k], hop_s.at[0], c_r.at[kind], tensor=t1)

    def hop_f(item):
        x, k, kind = place(item)
        return remote(x.at[2, k], x.at[3, k], hop_s.at[0], f_r.at[kind], tensor=t1)

    def all_c(x, kind):
        return remote(x.at[0], x.at[1], hop_s.at[0], c_r.at[kind], tensor=t1)

    def all_f(x, kind):
        return remote(x.at[2], x.at[3], hop_s.at[0], f_r.at[kind], tensor=t1)

    def hop_x(k):
        return remote(xb.at[0, k], xo.at[k], xo_s.at[0], xo_r.at[0], dp=1 - d)

    all_x = remote(xb.at[0], xo, xo_s.at[0], xo_r.at[0], dp=1 - d)

    def act(v, step):
        kind, item = step
        if kind in "sw":
            copy = gz if item[0] == "g" else az(v, item[1]) if item[0] == "a" else ex(v, item[1])
            copy.start() if kind == "s" else copy.wait_send()
            return
        if kind == "q":
            hop_y(item).wait_recv()
            hop_f(item).start()
            return
        if item[0] == "b":
            if item[1] != v:
                ex(item[1], v).wait_recv()
        elif v == 0:
            if item[1] == 0:
                emb_copy.wait()
        else:
            az(v - 1, item[1]).wait_recv()
        hop_y(item).start()
        hop_c(item).start()
        if item[0] == "b":
            hop_x(item[1]).start()

    def per_section(run):
        for v in range(S):
            pl.when(s == v)(functools.partial(run, v))

    def relay(slot):
        def run(v):
            for step in relay_slot(v, S, slot):
                act(v, step)
        per_section(run)

    def first_sends(v):
        act(v, ("p", ("b", v)))
        for k in first_targets(v, S):
            ex(v, k).start()
        if v == S - 1:
            loss_copy.start()
    per_section(first_sends)

    for r in range(4):
        d_copies[r].start()
        w_copies[r].start()
    up_copy.start()

    def run_rest(v):
        for step in relay_slot(v, S, 0):
            act(v, step)
    per_section(run_rest)

    def forward(x, r, acc):
        for n in range(tiles):
            val = dot_nn(x[r].reshape(rows, cols), w[r, :, pl.ds(n * tile, tile)])
            acc[n] = val if r == 0 else acc[n] + val

    def low_of(x, r):
        return dot_nn(x[r].reshape(rows, cols), dn[r])

    d_all.wait()
    w_copies[0].wait()
    forward(xb, 0, u)
    h = low_of(xb, 0)
    relay(1)
    all_c(xb, 1).wait_recv()
    w_copies[1].wait()
    forward(xb, 1, u)
    h = h + low_of(xb, 1)
    relay(2)
    w_copies[2].wait()
    forward(xb, 2, u)
    h = h + low_of(xb, 2)
    relay(3)
    all_f(xb, 1).wait_recv()
    w_copies[3].wait()
    forward(xb, 3, u)
    h = h + low_of(xb, 3)
    hb[...] = h.astype(BF16)
    relay(4)
    up_copy.wait()

    def slope_body(n, carry):
        at = pl.ds(pl.multiple_of(n * tile, tile), tile)
        unused, slope = gelu_pair(u[n] + dot_nn(hb[...], upv[:, at]))
        u[n] = slope
        return carry
    lax.fori_loop(0, tiles, slope_body, 0)
    relay(5)
    relay(6)

    def near_blocks():
        forward(xa, 0, ua)
        all_c(xa, 0).wait_recv()
        forward(xa, 1, ua)
    early = (s > 0) & (s < S // 2)
    pl.when(early)(near_blocks)
    relay(7)

    @pl.when(s == S - 1)
    def _():
        loss_copy.wait()

    @pl.when(s < S - 1)
    def _():
        gz.wait_recv()

    def scale_body(n, carry):
        at = pl.ds(pl.multiple_of(n * tile, tile), tile)
        scaled[:, at] = (g[:, :, at].reshape(rows, tile).astype(F32) * u[n]).astype(BF16)
        return carry
    lax.fori_loop(0, tiles, scale_body, 0)

    low_copy = remote(low, low_in, low_s.at[0], low_r.at[0], tensor=t1)
    share = rows // 2
    lower = pl.ds(pl.multiple_of((t % 2) * share, share), share)
    pair_copy = remote(pair.at[lower], pair_in.at[lower], low_s.at[1], low_r.at[1], tensor=t2)
    pair_hop = remote(pair_in.at[lower], pair_in.at[lower], low_s.at[2], low_r.at[2], tensor=t1)

    def partial(r, n):
        return dot_nt(scaled[...], w[r, pl.ds(n * part, part), :])

    def p_copy(n):
        return remote(p_send.at[n], p_recv.at[n], pqo_s.at[0], p_r.at[(n >= lead) + (n >= parts - lead)], tensor=t1)

    def p_group(group):
        at = pl.ds(group[0], len(group))
        which = (group[0] >= lead) + (group[0] >= parts - lead)
        return remote(p_send.at[at], p_recv.at[at], pqo_s.at[0], p_r.at[which], tensor=t1)

    def q_copy(n):
        return remote(q_send.at[n], q_recv.at[n], pqo_s.at[0], q_r.at[n], tensor=t2)

    def o_copy(n):
        return remote(o_send.at[n], o_recv.at[n], pqo_s.at[0], o_r.at[0], tensor=t1)

    lead = max(parts // 4, 1)
    first, second, third = range(lead), range(lead, parts - lead), range(parts - lead, parts)

    def p_step(group):
        for n in group:
            p_send[n] = partial(3, n).astype(BF16)
        for n in group:
            p_copy(n).start()

    def q_step(group):
        for n in group:
            own[n] = partial(2, n)
        p_group(group).wait_recv()
        for n in group:
            q_send[n] = (own[n] + p_recv[n].astype(F32)).astype(BF16)
        for n in group:
            q_copy(n).start()

    p_step(first)
    low[...] = dot_nt(scaled[...], upv[...]).astype(BF16)
    low_copy.start()
    relay(8)
    q_step(first)
    relay(9)
    p_step(second)
    du_send[...] = dot_tn(hb[...], scaled[...]).astype(BF16)
    du = remote(du_send, du_recv, dp_s.at[0], dp_r.at[0], dp=1 - d)
    du.start()
    low_copy.wait_recv()
    pair[...] = (low[...].astype(F32) + low_in[...].astype(F32)).astype(BF16)
    pair_copy.start()
    relay(12)

    def o_step(group):
        for n in group:
            o_send[n] = partial(1, n).astype(BF16)
        for n in group:
            o_copy(n).start()

    o_step(range(parts // 2))
    q_step(second)
    p_step(third)
    pl.when(jnp.logical_not(early))(near_blocks)
    relay(10)
    q_step(third)
    o_step(range(parts // 2, parts))
    relay(11)
    pair_copy.wait_recv()
    pair_hop.start()
    h = low_of(xa, 0) + low_of(xa, 1)
    forward(xa, 2, ua)
    h = h + low_of(xa, 2)
    pair_hop.wait_recv()
    lg[...] = (pair[...].astype(F32) + pair_in[...].astype(F32)).astype(BF16)
    dd = remote(lg, lg_in, dp_s.at[1], dp_r.at[1], dp=1 - d)
    dd.start()
    all_f(xa, 0).wait_recv()
    forward(xa, 3, ua)
    h = h + low_of(xa, 3)
    ha[...] = h.astype(BF16)

    def out_body(n, carry):
        at = pl.ds(pl.multiple_of(n * tile, tile), tile)
        value, unused = gelu_pair(ua[n] + dot_nn(ha[...], upv[:, at]))
        base = xa[0, :, :, at].reshape(rows, tile).astype(F32)
        out_f[:, at] = (base + value).astype(BF16)
        return carry
    lax.fori_loop(0, tiles, out_body, 0)
    keeps = [
        pltpu.make_async_copy(out_f, keep_f, keep_sem.at[0]),
        pltpu.make_async_copy(out_u, keep_u, keep_sem.at[1]),
        pltpu.make_async_copy(out_d, keep_d, keep_sem.at[2]),
    ]
    keeps[0].start()

    for n in range(parts):
        own[n] = partial(0, n) + dot_nt(lg[...], dn[0, pl.ds(n * part, part), :])

    du.wait_recv()
    out_u[...] = (du_send[...].astype(F32) + du_recv[...].astype(F32)).astype(BF16)
    keeps[1].start()

    all_x.wait_recv()
    dd.wait_recv()
    here = dot_tn(lg[...], xb[0].reshape(rows, cols))
    there = dot_tn(lg_in[...], xo[...].reshape(rows, cols))
    out_d[...] = (here + there).T.astype(BF16)
    keeps[2].start()

    remote(o_send, o_recv, pqo_s.at[0], o_r.at[0], tensor=t1).wait_recv()
    for n in range(parts):
        at = pl.ds(n * part, part)
        own[n] = own[n] + o_recv[n].astype(F32) + g[:, :, at].reshape(rows, part).astype(F32)

    def drain(v):
        for k in range(S):
            if k != v and ("w", ("b", k)) not in relay_slot(v, S, 0):
                ex(v, k).wait_send()
        if v < S - 1:
            remote(sent.at[1], xa.at[0], az_s.at[0], az_r.at[0], section=v + 1).wait_send()
        if v > 0:
            gz.wait_send()
    per_section(drain)
    all_x.wait_send()
    remote(xab.at[:, 0:3], xab.at[:, 1:4], hop_s.at[0], y_r.at[0], tensor=t1).wait_send()
    low_copy.wait_send()
    pair_copy.wait_send()
    pair_hop.wait_send()
    for n in range(parts):
        q_copy(n).wait_recv()
        at = pl.ds(n * part, part)
        out_b[:, at] = (own[n] + q_recv[n].astype(F32)).astype(BF16)
        pltpu.make_async_copy(out_b.at[:, at], keep_b.at[:, at], keep_sem.at[3]).start()

    remote(pqo_send, pqo_send, pqo_s.at[0], p_r.at[0], tensor=t1).wait_send()
    du.wait_send()
    dd.wait_send()
    for keep in keeps:
        keep.wait()
    pltpu.make_async_copy(out_b, keep_b, keep_sem.at[3]).wait()


def store_kernel(*refs):
    copies = [pltpu.make_async_copy(refs[i], refs[4 + i], refs[8].at[i]) for i in range(4)]
    for copy in copies:
        copy.start()
    for copy in copies:
        copy.wait()


def fused_on_device(sent, stash, table, embedded, loss, weight, down, up):
    S = lax.axis_size("section")
    piece, cols = stash.shape[1], stash.shape[2]
    rows, rank = S * piece, up.shape[1]
    tile = next(k for k in (768, 512, 256, 128) if cols % k == 0)
    part = next(k for k in (384, 256, 128) if cols % k == 0)
    tiles, parts = cols // tile, cols // part
    far = lambda x: pltpu.with_memory_space_constraint(x, pltpu.HBM)
    hbm = pl.BlockSpec(memory_space=pltpu.HBM)
    V = pltpu.VMEM
    dma = lambda *shape: pltpu.SemaphoreType.DMA(shape)
    block = (tiles, rows, tile)
    cut = (parts, rows, part)
    slim = V((rows, rank), BF16)
    stack = V((S, piece, cols), BF16)
    outs = pl.pallas_call(
        functools.partial(window_kernel, S, tile, part),
        out_shape=(
            jax.ShapeDtypeStruct((rows, cols), BF16),
            jax.ShapeDtypeStruct((rows, cols), BF16),
            jax.ShapeDtypeStruct((cols, rank), BF16),
            jax.ShapeDtypeStruct((rank, cols), BF16),
        ),
        in_specs=[hbm, hbm, hbm, hbm, hbm, hbm, hbm, hbm],
        out_specs=(pl.BlockSpec(memory_space=pl.ANY),) * 4,
        scratch_shapes=[
            V((rows, cols), BF16), V((rows, cols), BF16), V((cols, rank), BF16), V((rank, cols), BF16),
            pltpu.SMEM(table.shape, table.dtype), stack, V((4, cols, cols), BF16), V((4, cols, rank), BF16), V((rank, cols), BF16),
            V((2, 4, S, piece, cols), BF16),
            stack, stack,
            V(block, F32), V(block, F32), V((rows, cols), BF16),
            slim, slim, slim, slim, slim, slim, slim, slim,
            V((3,) + cut, BF16), V(cut, BF16), V(cut, BF16), V(cut, BF16), V(cut, F32),
            V((rank, cols), BF16), V((rank, cols), BF16), stack,
            dma(4), dma(1), dma(5), dma(4), dma(S), dma(S), dma(1), dma(S), dma(1), dma(1),
            dma(1), dma(1), dma(1), dma(2 * S), dma(2), dma(2), dma(3), dma(3), dma(1), dma(3), dma(parts), dma(1),
            dma(2), dma(2),
        ],
        compiler_params=pltpu.CompilerParams(
            collective_id=0, has_side_effects=True, vmem_limit_bytes=44 * 1024 * 1024),
    )(
        far(sent.reshape(2, S, piece, cols)), far(stash), far(table),
        far(embedded.reshape(S, piece, cols)), far(loss.reshape(S, piece, cols)),
        far(weight.reshape(4, cols, cols)), far(down.reshape(4, cols, rank)), far(up[0]),
    )
    stored = pl.pallas_call(
        store_kernel,
        out_shape=tuple(jax.ShapeDtypeStruct(o.shape, o.dtype) for o in outs),
        in_specs=[pl.BlockSpec(memory_space=pl.ANY)] * 4,
        out_specs=(hbm,) * 4,
        scratch_shapes=[dma(4)],
        compiler_params=pltpu.CompilerParams(vmem_limit_bytes=1024 * 1024),
    )(*outs)
    return tuple(o[None] for o in stored)


def solution(mesh):
    placed = (
        P("section", "dp", "tensor"),
        P("section", "dp", "tensor"),
        P("section", None),
        P("dp", "tensor"),
        P("dp", "tensor"),
        P("section", None, "tensor"),
        P("section", None, None),
        P("section", None, "tensor"),
    )
    def program(*args):
        rows = args[1].shape[1] // mesh.shape["dp"]
        cols = args[1].shape[2] // mesh.shape["tensor"]
        fits = (
            mesh.shape["tensor"] == 4 and mesh.shape["dp"] == 2
            and rows % 16 == 0 and cols % 128 == 0
        )
        return sharded(fused_on_device if fits else on_device)(*args)

    def sharded(body):
      return jax.shard_map(
        body,
        mesh=mesh,
        in_specs=placed,
        out_specs=(
            P("section", "dp", "tensor"),
            P("section", "dp", "tensor"),
            P("section", "tensor", None),
            P("section", None, "tensor"),
        ),
        check_vma=False,
    )

    return program
```
